32 devices in a mesh: dp: 16 (over z, y, x), head: 2 (over core).
Axes of the slice: x: 2, y: 2, z: 4, core: 2. Of those that a mesh axis runs over, the one named last changes fastest.
Arguments:
- tokens: bfloat16 [16384, 768], P(('dp', 'head')), may hold values from -6 to 6
- seq_len: int32 [32], P('dp'), may hold values from 128 to 512, as said below
- w_query: float32 [2, 768, 768], P(None, 'dp', 'head'), may hold values from -0.21875 to 0.21875
- w_key: float32 [2, 768, 768], P(None, 'dp', 'head'), may hold values from -0.21875 to 0.21875
- w_value: float32 [2, 768, 768], P(None, 'dp', 'head'), may hold values from -0.21875 to 0.21875
- w_out: float32 [2, 768, 768], P(None, ('dp', 'head')), may hold values from -0.875 to 0.875
- w_up: float32 [2, 768, 3072], P(None, ('dp', 'head')), may hold values from -0.21875 to 0.21875
- w_down: float32 [2, 3072, 768], P(None, ('dp', 'head')), may hold values from -0.109375 to 0.109375
- a_query: float32 [2, 768, 8], replicated, may hold values from -0.21875 to 0.21875
- b_query: float32 [2, 8, 768], P(None, None, 'head'), may hold values from -0.9 to 0.9
- a_value: float32 [2, 768, 8], replicated, may hold values from -0.21875 to 0.21875
- b_value: float32 [2, 8, 768], P(None, None, 'head'), may hold values from -0.9 to 0.9
- ln_gain: float32 [2, 2, 768], replicated, may hold values from 0.1 to 1.9
- ln_bias: float32 [2, 2, 768], replicated, may hold values from -1.5 to 1.5
- cotangent: bfloat16 [16384, 768], P(('dp', 'head')), may hold values from -6 to 6
Outputs:
- output: bfloat16 [16384, 768], P(('dp', 'head'))
- input_grad: float32 [16384, 768], P(('dp', 'head'))
- grad_a_query: float32 [2, 768, 8], replicated
- grad_b_query: float32 [2, 8, 768], P(None, None, 'head')
- grad_a_value: float32 [2, 768, 8], replicated
- grad_b_value: float32 [2, 8, 768], P(None, None, 'head')
The draws below stay inside these ranges and needn't reach their ends.
Inputs may be any that keep to these rules, and one draw needn't show every extreme that they name: Each block of 512 tokens holds whole sequences of length seq_len[block], which is a quarter of 512, half of it or all of it; the numbers of blocks of the three lengths differ by at most one.
All inputs are finite; a program needn't handle non-finite values.
Results may differ from the reference program's by a relative error of at most 0.028.
Values may be sent and summed in bfloat16 or wider, within the bound.
No kernel may reach another device: no remote copies, remote signals or barrier semaphores. Data moves between devices by JAX's collectives and lax.ppermute only.
A program may use at most 192 MiB of HBM per device.

```python
import jax
import jax.numpy as jnp
from jax import lax

D = 768
HEADS = 12
HEAD_DIM = 64
FF = 3072
RANK = 8
LAYERS = 2
BLOCK = 512
BLOCK_COUNT = 32
TOKENS = 16384
N_DP = 16


def draw_seq_len(key, part):
    order = jax.random.permutation(key, BLOCK_COUNT)
    bucket = order % 3
    return jnp.where(bucket == 0, BLOCK // 4, jnp.where(bucket == 1, BLOCK // 2, BLOCK)).astype(jnp.int32)


def levels(stream_key, extent, cuts, low, high):
    factor_of, own = 1.0, jax.random.fold_in(stream_key, 6)
    for dim, shards_of in cuts:
        heights = jnp.exp(jax.random.uniform(jax.random.fold_in(own, dim), (shards_of,), jnp.float32, low / len(cuts), high / len(cuts)))
        factor_of = factor_of * jnp.repeat(heights, extent[dim] // shards_of).reshape([-1 if axis == dim else 1 for axis in range(len(extent))])
    return factor_of


def bell_draw(rng, extent, width, bound, cuts=(), held_as=jnp.bfloat16):
    gain = levels(rng, extent, cuts, -0.22, 0.18) if cuts else 1.0
    drawn = jax.random.normal(rng, extent, jnp.float32) * width * gain
    return jnp.minimum(jnp.maximum(drawn, -bound), bound).astype(held_as)


def setup_inputs(seed: int = 0) -> dict:
    key_of = jax.random.split(jax.random.key(seed), 16)
    return {
        "tokens": bell_draw(key_of[0], (TOKENS, D), 1.0, 6.0, ((0, 32),)),
        "seq_len": draw_seq_len(jax.random.fold_in(key_of[15], 71), 0),
        "w_query": bell_draw(key_of[2], (LAYERS, D, D), D ** -0.5, 0.21875, ((1, 16), (2, 2)), jnp.float32),
        "w_key": bell_draw(key_of[3], (LAYERS, D, D), D ** -0.5, 0.21875, ((1, 16), (2, 2)), jnp.float32),
        "w_value": bell_draw(key_of[4], (LAYERS, D, D), D ** -0.5, 0.21875, ((1, 16), (2, 2)), jnp.float32),
        "w_out": bell_draw(key_of[5], (LAYERS, D, D), (D // 16) ** -0.5, 0.875, ((1, 32),), jnp.float32),
        "w_up": bell_draw(key_of[6], (LAYERS, D, FF), D ** -0.5, 0.21875, ((1, 32),), jnp.float32),
        "w_down": bell_draw(key_of[7], (LAYERS, FF, D), FF ** -0.5, 0.109375, ((1, 32),), jnp.float32),
        "a_query": bell_draw(key_of[8], (LAYERS, D, RANK), D ** -0.5, 0.21875, (), jnp.float32),
        "b_query": bell_draw(key_of[9], (LAYERS, RANK, D), 0.15, 0.9, ((2, 2),), jnp.float32),
        "a_value": bell_draw(key_of[10], (LAYERS, D, RANK), D ** -0.5, 0.21875, (), jnp.float32),
        "b_value": bell_draw(key_of[11], (LAYERS, RANK, D), 0.15, 0.9, ((2, 2),), jnp.float32),
        "ln_gain": jnp.clip(1.0 + 0.18 * jax.random.normal(key_of[12], (LAYERS, 2, D), jnp.float32), 0.1, 1.9),
        "ln_bias": bell_draw(key_of[13], (LAYERS, 2, D), 0.3, 1.5, (), jnp.float32),
        "cotangent": bell_draw(key_of[14], (TOKENS, D), 1.0, 6.0, ((0, 32),)),
    }


epsilon = 1e-05

@jax.custom_vjp
def low(v):
    return lax.optimization_barrier(v.astype(jnp.bfloat16)).astype(jnp.float32)

@jax.custom_vjp
def low_back(v):
    return v

def low_keep(v):
    return (low(v), None)

def low_pass(kept, grad):
    return (grad,)

def back_keep(v):
    return (v, None)

def back_low(kept, grad):
    return (low(grad),)
low.defvjp(low_keep, low_pass)
low_back.defvjp(back_keep, back_low)

def exact_dot(left, right):
    return jnp.dot(left, right, precision=lax.Precision.HIGHEST)

def layer_norm(values, gain_row, offset_row):
    center = values - lax.optimization_barrier(jnp.mean(values, -1, keepdims=True))
    spread = lax.optimization_barrier(jnp.mean(center * center, -1, keepdims=True))
    return center * lax.rsqrt(spread + epsilon) * gain_row + offset_row

def attend_block(pieces):
    queries, key_rows, value_rows, length = pieces
    row_count = queries.shape[0]
    head_shape = (row_count, HEADS, HEAD_DIM)
    head_q = queries.reshape(head_shape)
    head_k = key_rows.reshape(head_shape)
    head_v = value_rows.reshape(head_shape)
    scores = jnp.einsum('qhd,khd->hqk', head_q, head_k, precision=lax.Precision.HIGHEST) * HEAD_DIM ** (-0.5)
    scores = low_back(scores)
    segment = lax.iota(jnp.int32, row_count) // length
    allowed = segment[:, None] == segment[None, :]
    scores = jnp.where(allowed[None], scores, -1e+30)
    largest = lax.optimization_barrier(jnp.max(scores, -1, keepdims=True))
    raised = jnp.exp(scores - largest)
    weights_now = low(raised / lax.optimization_barrier(jnp.sum(raised, -1, keepdims=True)))
    mixed_rows = jnp.einsum('hqk,khd->qhd', weights_now, head_v, precision=lax.Precision.HIGHEST)
    return mixed_rows.reshape(row_count, HEADS * HEAD_DIM)

def attend(queries, key_rows, value_rows, lengths):
    blocks = lengths.shape[0]
    block_shape = (blocks, queries.shape[0] // blocks, queries.shape[1])
    mixed_rows = lax.map(jax.checkpoint(attend_block), (queries.reshape(block_shape), key_rows.reshape(block_shape), value_rows.reshape(block_shape), lengths))
    return mixed_rows.reshape(queries.shape)

def group_forward(stream, adapters, frozen, lengths):
    a_query, b_query, a_value, b_value = adapters
    w_query, w_key, w_value, w_out, w_up, w_down, ln_gain, ln_bias = frozen
    for layer_at in range(LAYERS):
        rounded = low(stream)
        mid_query = low(exact_dot(rounded, a_query[layer_at]))
        mid_value = low(exact_dot(rounded, a_value[layer_at]))
        queries = low(low_back(exact_dot(rounded, w_query[layer_at]) + 2.0 * exact_dot(mid_query, b_query[layer_at])))
        key_rows = low(low_back(exact_dot(rounded, w_key[layer_at])))
        value_rows = low(low_back(exact_dot(rounded, w_value[layer_at]) + 2.0 * exact_dot(mid_value, b_value[layer_at])))
        attended = low(low_back(attend(queries, key_rows, value_rows, lengths)))
        hidden = stream + low_back(exact_dot(attended, w_out[layer_at]))
        normed = layer_norm(hidden, ln_gain[layer_at, 0], ln_bias[layer_at, 0])
        pre_act = low_back(exact_dot(low(normed), w_up[layer_at]))
        activated = low(jax.nn.gelu(pre_act, approximate=False))
        second = normed + low_back(exact_dot(activated, w_down[layer_at]))
        stream = layer_norm(second, ln_gain[layer_at, 1], ln_bias[layer_at, 1])
    return stream

def reference(tokens, seq_len, w_query, w_key, w_value, w_out, w_up, w_down, a_query, b_query, a_value, b_value, ln_gain, ln_bias, cotangent):
    frozen = (low(w_query), low(w_key), low(w_value), low(w_out), low(w_up), low(w_down), ln_gain, ln_bias)
    group_rows = tokens.shape[0] // N_DP
    streams = tokens.astype(jnp.float32).reshape(N_DP, group_rows, D)
    upstream = cotangent.astype(jnp.float32).reshape(N_DP, group_rows, D)
    lengths = seq_len.reshape(N_DP, -1)
    adapters = (a_query, b_query, a_value, b_value)

    def one_group(totals, pieces):
        stream, grad_in, group_lengths = pieces
        result, pullback = jax.vjp(lambda values, params: group_forward(values, params, frozen, group_lengths), stream, adapters)
        grad_stream, grad_params = pullback(grad_in)
        totals = jax.tree.map(lambda held_sum, fresh_sum: held_sum + fresh_sum, totals, grad_params)
        return (totals, (result.astype(jnp.bfloat16), grad_stream))
    initial = jax.tree.map(jnp.zeros_like, adapters)
    totals, (results, grad_rows) = lax.scan(one_group, initial, (streams, upstream, lengths))
    return (results.reshape(tokens.shape), grad_rows.reshape(tokens.shape), totals[0], totals[1], totals[2], totals[3])
```

```python
import functools

import jax
import jax.numpy as jnp
from jax import lax
from jax.experimental import pallas as pl
from jax.experimental.pallas import tpu as pltpu
from jax.sharding import PartitionSpec as P

HEAD_DIM = 64
EPS = 1e-05
BF = jnp.bfloat16
F32 = jnp.float32
TAIL_T = 0.3
TAIL_POLY = (
    0.11962930085896954,
    0.12075392575453824,
    0.09991367489054633,
    0.1285610470550418,
    -0.0536825996264651,
    0.20635243353234553,
    -0.1572025001665815,
    0.03567464489776359,
)
PHI_SCALE = 0.3989422804014327
VMEM_LIMIT = 60 * 1024 * 1024


def mm(left, right):
    return lax.dot_general(left, right, (((1,), (0,)), ((), ())), preferred_element_type=F32)


def mm_rt(left, right):
    return lax.dot_general(left, right, (((1,), (1,)), ((), ())), preferred_element_type=F32)


def mm_lt(left, right):
    return lax.dot_general(left, right, (((0,), (0,)), ((), ())), preferred_element_type=F32)


def chip_grid(count):
    side = round((count / 2) ** (1 / 3))
    if 2 * side**3 == count:
        return (2 * side, side, side)
    return (count, 1, 1)


def shift(values, grid, axis, by):
    nz, ny, nx = grid
    pairs = []
    for z in range(nz):
        for y in range(ny):
            for x in range(nx):
                to = [z, y, x]
                to[axis] = (to[axis] + by) % grid[axis]
                pairs.append(((z * ny + y) * nx + x, (to[0] * ny + to[1]) * nx + to[2]))
    return lax.ppermute(values, "dp", pairs)


def swap_cores(values):
    size = lax.axis_size("head")
    return lax.ppermute(values, "head", [(i, (i + 1) % size) for i in range(size)])


def after(values, *earlier):
    return lax.optimization_barrier((values, *earlier))[0]


def spread_z(packed, grid):
    return [packed] + [shift(packed, grid, 0, k) for k in range(1, grid[0])]


def spread_yx(part, grid, first, second):
    lines = jnp.stack([part] + [shift(part, grid, first, k) for k in range(1, grid[first])])
    return [lines] + [shift(lines, grid, second, k) for k in range(1, grid[second])]


def copy_list(grid, a_refs, b_refs, a_jobs, b_jobs, sem):
    nz, ny, nx = grid
    dp = lax.axis_index("dp")
    core = lax.axis_index("head")
    z, y, x = dp // (ny * nx), (dp // nx) % ny, dp % nx
    for refs, jobs, first_is_y in ((a_refs, a_jobs, True), (b_refs, b_jobs, False)):
        if not jobs:
            continue
        for last, pair in enumerate(refs):
            for other in range(2):
                ref = pair[other]
                c = core if other == 0 else 1 - core
                for first in range(ref.shape[0]):
                    for kz in range(nz):
                        zz = lax.rem(z + nz - kz, nz)
                        if first_is_y:
                            yy, xx = lax.rem(y + ny - first, ny), lax.rem(x + nx - last, nx)
                        else:
                            yy, xx = lax.rem(y + ny - last, ny), lax.rem(x + nx - first, nx)
                        owner = (zz * ny + yy) * nx + xx
                        for job in jobs:
                            job(ref.at[first, kz], owner, c, sem)


def job_cols(dst, rows, lane0, width, col0):
    def run(src, owner, c, sem):
        row = pl.multiple_of(owner * rows, 16)
        col = pl.multiple_of(col0 + c * width, 128)
        pltpu.make_async_copy(
            src.at[:, pl.ds(lane0, width)], dst.at[pl.ds(row, rows), pl.ds(col, width)], sem
        ).start()

    return run


def job_rows(dst, rows, parts, part, lane0):
    def run(src, owner, c, sem):
        row = pl.multiple_of(((owner * 2 + c) * parts + part) * rows, 16)
        width = dst.shape[1]
        pltpu.make_async_copy(
            src.at[:, pl.ds(lane0 + part * width, width)], dst.at[pl.ds(row, rows), :], sem
        ).start()

    return run


def wait_all(dst, sem):
    pltpu.make_async_copy(dst, dst, sem).wait()


class Weights:
    def __init__(self, grid, arrays):
        self.grid = grid
        self.arrays = arrays

    def flat(self, names):
        leaves = []
        for name in names:
            leaves += jax.tree.leaves(self.arrays[name])
        return leaves

    def unflat(self, names, refs):
        out, at = {}, 0
        for name in names:
            leaves, tree = jax.tree.flatten(self.arrays[name])
            out[name] = jax.tree.unflatten(tree, refs[at : at + len(leaves)])
            at += len(leaves)
        return out, refs[at:]


def start_qkv(grid, refs, dst, sem):
    if "qkv" in refs:
        pltpu.make_async_copy(refs["qkv"], dst, sem).start()
        return
    rows, half = refs["qk"][0][0].shape[2], dst.shape[1] // 6
    copy_list(
        grid,
        refs["qk"],
        refs["v"],
        (job_cols(dst, rows, 0, half, 0), job_cols(dst, rows, half, half, 2 * half)),
        (job_cols(dst, rows, 0, half, 4 * half),),
        sem,
    )


def start_out(grid, refs, dst, sem):
    if "out" in refs:
        pltpu.make_async_copy(refs["out"], dst, sem).start()
        return
    ref = refs["rest"][0][0]
    rows, half = ref.shape[2], dst.shape[1] // 2
    copy_list(
        grid, (), refs["rest"], (), (job_cols(dst, rows, ref.shape[3] - half, half, 0),), sem
    )


def start_up(grid, refs, dst, sem):
    if "out" in refs:
        pltpu.make_async_copy(refs["up"], dst, sem).start()
        return
    rows, half = refs["up"][0][0].shape[2], dst.shape[1] // 2
    copy_list(grid, refs["up"], (), (job_cols(dst, rows, 0, half, 0),), (), sem)


def start_down(grid, refs, dst, sem):
    if "out" in refs:
        pltpu.make_async_copy(refs["down"], dst, sem).start()
        return
    ref = refs["rest"][0][0]
    rows = ref.shape[2]
    parts = ref.shape[3] // dst.shape[1]
    jobs = tuple(job_rows(dst, rows, parts, i, 0) for i in range(parts))
    copy_list(grid, (), refs["rest"], (), jobs, sem)


QKV_NAMES = {True: ("qk", "v"), False: ("qkv",)}
DENSE_NAMES = {True: ("up", "rest"), False: ("out", "up", "down")}


def kernel_call(body, outs, scratch, flops, ins_vmem, ins_any, scalar):
    specs = [pl.BlockSpec(memory_space=pltpu.SMEM)] * len(scalar)
    specs += [pl.BlockSpec(memory_space=pltpu.VMEM)] * len(ins_vmem)
    specs += [pl.BlockSpec(memory_space=pl.ANY)] * len(ins_any)
    moved = sum(v.size * v.dtype.itemsize for v in (*ins_vmem, *ins_any, *outs))
    return pl.pallas_call(
        body,
        out_shape=tuple(outs),
        in_specs=specs,
        out_specs=tuple([pl.BlockSpec(memory_space=pltpu.VMEM)] * len(outs)),
        scratch_shapes=scratch,
        compiler_params=pltpu.CompilerParams(vmem_limit_bytes=VMEM_LIMIT),
        cost_estimate=pl.CostEstimate(flops=flops, bytes_accessed=moved, transcendentals=0),
    )(*scalar, *ins_vmem, *ins_any)


def sds(shape, dtype):
    return jax.ShapeDtypeStruct(shape, dtype)


def mask_bias(length, rows):
    near = lax.broadcasted_iota(jnp.int32, (rows, rows), 0) // length
    far = lax.broadcasted_iota(jnp.int32, (rows, rows), 1) // length
    return jnp.where(near == far, 0.0, -1e30).astype(F32)


def block_length(len_ref):
    return len_ref[lax.axis_index("head")]


def attend_forward(x, down, up, weights, pieces, lengths):
    rows, width = x.shape
    names = QKV_NAMES[pieces]
    wide = 3 * width
    pairs = width // 128

    def body(len_ref, x_ref, down_ref, up_ref, *rest):
        refs, rest = weights.unflat(names, rest)
        q_ref, k_ref, v_ref, o_ref, lse_ref, mid_ref, w_ref, bias_ref, sem = rest
        start_qkv(weights.grid, refs, w_ref, sem)
        r = x_ref[...].astype(BF)
        mid = mm(r, down_ref[...]).astype(BF)
        mid_ref[...] = mid
        bias_ref[...] = mask_bias(block_length(len_ref), rows)
        wait_all(w_ref, sem)
        tile = 256
        for at, out in enumerate((q_ref, k_ref, v_ref)):
            for j in range(0, width, tile):
                c = at * width + j
                total = mm(r, w_ref[:, c : c + tile])
                if at != 1:
                    total += mm(mid, up_ref[:, c : c + tile])
                out[:, j : j + tile] = total.astype(BF)

        lane = lax.broadcasted_iota(jnp.int32, (rows, 128), 1)
        low = lane < HEAD_DIM
        zero = jnp.zeros((rows, 128), BF)
        one_low = jnp.where(low, 1.0, 0.0).astype(BF)
        one_high = jnp.where(low, 0.0, 1.0).astype(BF)

        def pair(p, carry):
            lanes = pl.ds(pl.multiple_of(p * 128, 128), 128)
            q2 = q_ref[:, lanes] * 0.125
            k2 = k_ref[:, lanes]
            v2 = v_ref[:, lanes]
            bias = bias_ref[...]
            s0 = mm_rt(q2, jnp.where(low, k2, zero)) + bias
            s1 = mm_rt(q2, jnp.where(low, zero, k2)) + bias
            m0 = jnp.max(s0, -1, keepdims=True)
            m1 = jnp.max(s1, -1, keepdims=True)
            e0 = jnp.exp(s0 - m0).astype(BF)
            e1 = jnp.exp(s1 - m1).astype(BF)
            v0 = jnp.concatenate([jnp.where(low, v2, zero), one_low], 1)
            v1 = jnp.concatenate([jnp.where(low, zero, v2), one_high], 1)
            both = mm(e0, v0) + mm(e1, v1)
            total = both[:, 128:]
            o_ref[:, lanes] = (both[:, :128] / total).astype(BF)
            lse = jnp.where(low, m0, m1) + jnp.log(total)
            flip = lse.T
            lse_ref[2 * p] = flip[0:8]
            lse_ref[2 * p + 1] = flip[64:72]
            return carry

        lax.fori_loop(0, pairs, pair, 0)

    act = sds((rows, width), BF)
    outs = (act, act, act, act, sds((2 * pairs, 8, rows), F32), sds((rows, 128), BF))
    flops = 2 * rows * width * wide + 4 * rows * rows * width * 4
    return kernel_call(
        body,
        outs,
        [
            pltpu.VMEM((width, wide), BF),
            pltpu.VMEM((rows, rows), F32),
            pltpu.SemaphoreType.DMA,
        ],
        flops,
        (x, down, up),
        weights.flat(names),
        (lengths,),
    )


def normalize(values):
    center = values - jnp.mean(values, -1, keepdims=True)
    scale = lax.rsqrt(jnp.mean(center * center, -1, keepdims=True) + EPS)
    return center * scale, scale


def gelu_pair(u):
    size = jnp.abs(u)
    t = 1.0 / (1.0 + TAIL_T * size)
    bell = jnp.exp(-0.5 * (u * u))
    poly = jnp.full_like(u, TAIL_POLY[-1])
    for coef in TAIL_POLY[-2::-1]:
        poly = poly * t + coef
    tail = poly * (t * bell)
    value = jnp.maximum(u, 0.0) - size * tail
    slope = jnp.where(u < 0.0, tail, 1.0 - tail) + u * (bell * PHI_SCALE)
    return value, slope


def dense_forward(x, attended, rows8, weights, pieces, out_type):
    rows, width = x.shape
    ff = weights.ff
    names = DENSE_NAMES[pieces]
    tile = 256

    def body(x_ref, o_ref, rows_ref, *rest):
        refs, rest = weights.unflat(names, rest)
        out_ref, n1_ref, n2_ref, rs_ref, slope_ref, wo_ref, wu_ref, wd_ref, y_ref, z_ref, sem = rest
        start_out(weights.grid, refs, wo_ref, sem.at[0])
        start_up(weights.grid, refs, wu_ref, sem.at[1])
        start_down(weights.grid, refs, wd_ref, sem.at[2])
        wait_all(wo_ref, sem.at[0])
        hid = x_ref[...].astype(F32) + mm(o_ref[...], wo_ref[...])
        n1, rs1 = normalize(hid)
        n1_ref[...] = n1.astype(BF)
        y = n1 * rows_ref[0:1] + rows_ref[1:2]
        z_ref[...] = y
        y_ref[...] = y.astype(BF)
        wait_all(wu_ref, sem.at[1])
        wait_all(wd_ref, sem.at[2])

        def step(j, carry):
            cols = pl.ds(pl.multiple_of(j * tile, tile), tile)
            u = mm(y_ref[...], wu_ref[:, cols])
            value, slope = gelu_pair(u)
            slope_ref[:, cols] = slope.astype(BF)
            z_ref[...] += mm(value.astype(BF), wd_ref[cols, :])
            return carry

        lax.fori_loop(0, ff // tile, step, 0)
        n2, rs2 = normalize(z_ref[...])
        n2_ref[...] = n2.astype(BF)
        lane = lax.broadcasted_iota(jnp.int32, (rows, 128), 1)
        rs_ref[...] = jnp.where(lane < 64, rs1, rs2)
        out_ref[...] = (n2 * rows_ref[2:3] + rows_ref[3:4]).astype(out_type)

    outs = (
        sds((rows, width), out_type),
        sds((rows, width), BF),
        sds((rows, width), BF),
        sds((rows, 128), F32),
        sds((rows, ff), BF),
    )
    flops = 2 * rows * width * (width + 2 * ff)
    return kernel_call(
        body,
        outs,
        [
            pltpu.VMEM((width, width), BF),
            pltpu.VMEM((width, ff), BF),
            pltpu.VMEM((ff, width), BF),
            pltpu.VMEM((rows, width), BF),
            pltpu.VMEM((rows, width), F32),
            pltpu.SemaphoreType.DMA((3,)),
        ],
        flops,
        (x, attended, rows8),
        weights.flat(names),
        (),
    )


def norm_backward(gn, n, scale):
    return (gn - jnp.mean(gn, -1, keepdims=True) - n * jnp.mean(gn * n, -1, keepdims=True)) * scale


def dense_backward(g, saved, rows8, weights, pieces):
    n1, n2, rs, slope = saved
    rows, width = g.shape
    ff = weights.ff
    names = DENSE_NAMES[pieces]
    tile = 256

    def body(g_ref, n1_ref, n2_ref, rs_ref, slope_ref, rows_ref, *rest):
        refs, rest = weights.unflat(names, rest)
        ghid_ref, go_ref, wo_ref, wu_ref, wd_ref, gz_ref, gy_ref, sem = rest
        start_down(weights.grid, refs, wd_ref, sem.at[2])
        start_up(weights.grid, refs, wu_ref, sem.at[1])
        start_out(weights.grid, refs, wo_ref, sem.at[0])
        gn = g_ref[...].astype(F32) * rows_ref[2:3]
        gz = norm_backward(gn, n2_ref[...].astype(F32), rs_ref[:, 64:65])
        gz_ref[...] = gz.astype(BF)
        gy_ref[...] = gz
        wait_all(wd_ref, sem.at[2])
        wait_all(wu_ref, sem.at[1])

        def step(j, carry):
            cols = pl.ds(pl.multiple_of(j * tile, tile), tile)
            ga = mm_rt(gz_ref[...], wd_ref[cols, :])
            gu = (ga * slope_ref[:, cols].astype(F32)).astype(BF)
            gy_ref[...] += mm_rt(gu, wu_ref[:, cols])
            return carry

        lax.fori_loop(0, ff // tile, step, 0)
        gn1 = gy_ref[...] * rows_ref[0:1]
        ghid = norm_backward(gn1, n1_ref[...].astype(F32), rs_ref[:, 0:1])
        ghid_ref[...] = ghid
        wait_all(wo_ref, sem.at[0])
        go_ref[...] = mm_rt(ghid.astype(BF), wo_ref[...]).astype(BF)

    outs = (sds((rows, width), F32), sds((rows, width), BF))
    flops = 2 * rows * width * (width + 2 * ff)
    return kernel_call(
        body,
        outs,
        [
            pltpu.VMEM((width, width), BF),
            pltpu.VMEM((width, ff), BF),
            pltpu.VMEM((ff, width), BF),
            pltpu.VMEM((rows, width), BF),
            pltpu.VMEM((rows, width), F32),
            pltpu.SemaphoreType.DMA((3,)),
        ],
        flops,
        (g, n1, n2, rs, slope, rows8),
        weights.flat(names),
        (),
    )


def attend_backward(saved, go, lengths):
    q, k, v, o, lse = saved
    rows, width = q.shape
    pairs = width // 128

    def body(len_ref, q_ref, k_ref, v_ref, o_ref, go_ref, lse_ref, gq_ref, gk_ref, gv_ref, bias_ref):
        bias_ref[...] = mask_bias(block_length(len_ref), rows)
        low = lax.broadcasted_iota(jnp.int32, (rows, 128), 1) < HEAD_DIM
        zero = jnp.zeros((rows, 128), BF)
        side = lax.broadcasted_iota(jnp.int32, (16, 128), 0) < 8
        pick = (side == (lax.broadcasted_iota(jnp.int32, (16, 128), 1) < HEAD_DIM)).astype(F32)

        def pair(p, carry):
            lanes = pl.ds(pl.multiple_of(p * 128, 128), 128)
            q2 = q_ref[:, lanes] * 0.125
            k2 = k_ref[:, lanes]
            v2 = v_ref[:, lanes]
            go2 = go_ref[:, lanes]
            prod = go2.astype(F32) * o_ref[:, lanes].astype(F32)
            dots = lax.dot_general(
                pick,
                prod,
                (((1,), (1,)), ((), ())),
                precision=lax.Precision.HIGHEST,
                preferred_element_type=F32,
            )
            gq = jnp.zeros((rows, 128), F32)
            gk = jnp.zeros((rows, 128), F32)
            gv = jnp.zeros((rows, 128), F32)
            for h in range(2):
                keep = (lambda t: jnp.where(low, t, zero)) if h == 0 else (lambda t: jnp.where(low, zero, t))
                qh, kh, goh = keep(q2), keep(k2), keep(go2)
                s = mm_rt(k2, qh) + bias_ref[...]
                prob = jnp.exp(s - lse_ref[2 * p + h][0:1])
                gp = mm_rt(v2, goh)
                gs = (prob * (gp - dots[8 * h : 8 * h + 1])).astype(BF)
                gq += mm_lt(gs, kh)
                gk += mm(gs, qh)
                gv += mm(prob.astype(BF), goh)
            gq_ref[:, lanes] = (gq * 0.125).astype(BF)
            gk_ref[:, lanes] = gk.astype(BF)
            gv_ref[:, lanes] = gv.astype(BF)
            return carry

        lax.fori_loop(0, pairs, pair, 0)

    act = sds((rows, width), BF)
    return kernel_call(
        body,
        (act, act, act),
        [pltpu.VMEM((rows, rows), F32)],
        20 * rows * rows * width,
        (q, k, v, o, go, lse),
        (),
        (lengths,),
    )


def adapter_grads(x, mid, gq, gv, up):
    rows, width = x.shape

    def body(x_ref, mid_ref, gq_ref, gv_ref, up_ref, gm_ref, sums_ref):
        gq, gv, mid = gq_ref[...], gv_ref[...], mid_ref[...]
        gm = mm_rt(gq, up_ref[:, :width]) + mm_rt(gv, up_ref[:, 2 * width :])
        gm = gm.astype(BF)
        gm_ref[...] = gm
        sums_ref[0:16] = mm_lt(gm, x_ref[...].astype(BF))[0:16]
        sums_ref[16:24] = 2.0 * mm_lt(mid, gq)[0:8]
        sums_ref[24:32] = 2.0 * mm_lt(mid, gv)[8:16]

    return kernel_call(
        body,
        (sds((rows, 128), BF), sds((32, width), F32)),
        [],
        2 * rows * width * 128 * 5,
        (x, mid, gq, gv, up),
        (),
        (),
    )


def input_grad(ghid, gq, gk, gv, gm, down, weights, pieces):
    rows, width = ghid.shape
    names = QKV_NAMES[pieces]

    def body(ghid_ref, gq_ref, gk_ref, gv_ref, gm_ref, down_ref, *rest):
        refs, rest = weights.unflat(names, rest)
        out_ref, w_ref, sem = rest
        start_qkv(weights.grid, refs, w_ref, sem)
        total = ghid_ref[...] + mm_rt(gm_ref[...], down_ref[...])
        wait_all(w_ref, sem)
        total += mm_rt(gq_ref[...], w_ref[:, :width])
        total += mm_rt(gk_ref[...], w_ref[:, width : 2 * width])
        total += mm_rt(gv_ref[...], w_ref[:, 2 * width :])
        out_ref[...] = total

    return kernel_call(
        body,
        (sds((rows, width), F32),),
        [pltpu.VMEM((width, 3 * width), BF), pltpu.SemaphoreType.DMA],
        6 * rows * width * width,
        (ghid, gq, gk, gv, gm, down),
        weights.flat(names),
        (),
    )[0]


def gather_pieces(grid, packs, halves):
    gathered = []
    gate = None
    for packed, (cut_a, cut_b) in zip(packs, halves):
        if gate is not None:
            packed = after(packed, *gate)
        line = spread_z(packed, grid)
        gate = line[1:]
        a_part = jnp.stack([cut_a(piece) for piece in line])
        b_part = jnp.stack([cut_b(piece) for piece in line])
        a_all = spread_yx(a_part, grid, 1, 2)
        b_all = spread_yx(b_part, grid, 2, 1)
        gathered.append(
            (
                [(own, swap_cores(own)) for own in a_all],
                [(own, swap_cores(own)) for own in b_all],
            )
        )
    return gathered


def all_weights(grid, w_query, w_key, w_value, w_out, w_up, w_down):
    layers = w_query.shape[0]
    ff = w_up.shape[2]
    half = w_query.shape[2]
    width = 2 * half
    pieces = w_query.shape[1] % 16 == 0 and lax.axis_size("head") == 2
    everything = []
    if not pieces:
        for at in range(layers):
            qkv = jnp.concatenate([w[at].astype(BF) for w in (w_query, w_key, w_value)], 1)
            qkv = lax.all_gather(qkv, "dp", axis=0, tiled=True)
            qkv = lax.all_gather(qkv, "head", axis=0, tiled=False)
            qkv = qkv.reshape(-1, width, 3, half).transpose(1, 2, 0, 3).reshape(width, 3 * width)
            rest = [
                lax.all_gather(w[at].astype(BF), ("dp", "head"), axis=0, tiled=True)
                for w in (w_out, w_up, w_down)
            ]
            layer = Weights(grid, {"qkv": qkv, "out": rest[0], "up": rest[1], "down": rest[2]})
            layer.ff = ff
            everything.append(layer)
        return pieces, everything
    core = lax.axis_index("head")
    both = jnp.concatenate([w_out, w_up], 2).astype(BF)
    mine = [lax.dynamic_slice_in_dim(both, core * half, half, 2)]
    mine += [lax.dynamic_slice_in_dim(both, width + core * (ff // 2), ff // 2, 2)]
    send = [lax.dynamic_slice_in_dim(both, (1 - core) * half, half, 2)]
    send += [lax.dynamic_slice_in_dim(both, width + (1 - core) * (ff // 2), ff // 2, 2)]
    mine = jnp.concatenate(mine, 2)
    come = swap_cores(jnp.concatenate(send, 2))
    both = jnp.concatenate([jnp.where(core == 0, mine, come), jnp.where(core == 0, come, mine)], 1)
    packs, halves = [], []
    rows = w_query.shape[1]
    for at in range(layers):
        packs.append(
            jnp.concatenate([w[at].astype(BF) for w in (w_query, w_key, w_value)], 1)
        )
        halves.append((lambda t: t[:, :width], lambda t: t[:, width:]))
        wd = w_down[at].astype(BF)
        wd = [wd[i : i + rows] for i in range(0, wd.shape[0], rows)]
        packs.append(jnp.concatenate([both[at, :, half:], *wd, both[at, :, :half]], 1))
        halves.append((lambda t: t[:, : ff // 2], lambda t: t[:, ff // 2 :]))
    gathered = gather_pieces(grid, packs, halves)
    for at in range(layers):
        attn, dense = gathered[2 * at], gathered[2 * at + 1]
        layer = Weights(grid, {"qk": attn[0], "v": attn[1], "up": dense[0], "rest": dense[1]})
        layer.ff = ff
        everything.append(layer)
    return pieces, everything


def sum_over_devices(sums, grid):
    half = sums.shape[1] // 2
    core = lax.axis_index("head")
    mine = lax.dynamic_slice_in_dim(sums, core * half, half, 1)
    other = lax.dynamic_slice_in_dim(sums, (1 - core) * half, half, 1)
    total = mine + swap_cores(other)
    for axis in (2, 1, 0):
        parts = [total] + [shift(total, grid, axis, k) for k in range(1, grid[axis])]
        total = functools.reduce(jnp.add, parts)
    return total


def body(
    tokens,
    seq_len,
    w_query,
    w_key,
    w_value,
    w_out,
    w_up,
    w_down,
    a_query,
    b_query,
    a_value,
    b_value,
    ln_gain,
    ln_bias,
    cotangent,
):
    layers, width = w_query.shape[0], tokens.shape[1]
    rank = a_query.shape[2]
    half = b_query.shape[2]
    grid = chip_grid(lax.axis_size("dp"))
    core = lax.axis_index("head")
    pieces, weights = all_weights(grid, w_query, w_key, w_value, w_out, w_up, w_down)

    own = jnp.stack([b_query, b_value], 1).astype(BF)
    other = swap_cores(own)
    up_all = jnp.concatenate(
        [jnp.where(core == 0, own, other), jnp.where(core == 0, other, own)], -1
    )
    downs, ups, rows8 = [], [], []
    for at in range(layers):
        pair = jnp.concatenate([a_query[at], a_value[at]], 1).astype(BF)
        downs.append(jnp.pad(pair, ((0, 0), (0, 128 - 2 * rank))))
        q_up = jnp.pad(2.0 * up_all[at, 0], ((0, 128 - rank), (0, 0)))
        v_up = jnp.pad(2.0 * up_all[at, 1], ((rank, 128 - 2 * rank), (0, 0)))
        ups.append(jnp.concatenate([q_up, jnp.zeros_like(q_up), v_up], 1))
        rows8.append(
            jnp.pad(
                jnp.stack([ln_gain[at, 0], ln_bias[at, 0], ln_gain[at, 1], ln_bias[at, 1]]),
                ((0, 4), (0, 0)),
            )
        )

    stream = tokens
    saved = []
    for at in range(layers):
        q, k, v, o, lse, mid = attend_forward(stream, downs[at], ups[at], weights[at], pieces, seq_len)
        last = at == layers - 1
        result, n1, n2, rs, slope = dense_forward(
            stream, o, rows8[at], weights[at], pieces, BF if last else F32
        )
        saved.append((stream, mid, (q, k, v, o, lse), (n1, n2, rs, slope)))
        stream = result
    output = stream
    grad = cotangent
    sums = [None] * layers
    for at in reversed(range(layers)):
        x, mid, attn, dense = saved[at]
        ghid, go = dense_backward(grad, dense, rows8[at], weights[at], pieces)
        gq, gk, gv = attend_backward(attn, go, seq_len)
        gm, sums[at] = adapter_grads(x, mid, gq, gv, ups[at])
        grad = input_grad(ghid, gq, gk, gv, gm, downs[at], weights[at], pieces)
    total = sum_over_devices(jnp.concatenate(sums, 0), grid).reshape(layers, 4, rank, half)
    lower = total[:, :2].reshape(layers * 2 * rank, half)
    far = swap_cores(lower)
    lower = jnp.concatenate([jnp.where(core == 0, lower, far), jnp.where(core == 0, far, lower)], 1)
    lower = lower.reshape(layers, 2, rank, width).transpose(0, 1, 3, 2)
    return (output, grad, lower[:, 0], total[:, 2], lower[:, 1], total[:, 3])


def solution(mesh):
    both = ("dp", "head")
    placed = (
        P(both, None),
        P("dp"),
        P(None, "dp", "head"),
        P(None, "dp", "head"),
        P(None, "dp", "head"),
        P(None, both, None),
        P(None, both, None),
        P(None, both, None),
        P(),
        P(None, None, "head"),
        P(),
        P(None, None, "head"),
        P(),
        P(),
        P(both, None),
    )
    return jax.shard_map(
        body,
        mesh=mesh,
        in_specs=placed,
        out_specs=(
            P(both, None),
            P(both, None),
            P(),
            P(None, None, "head"),
            P(),
            P(None, None, "head"),
        ),
        check_vma=False,
    )
```

```python
import functools

import jax
import jax.numpy as jnp
from jax import lax
from jax.experimental import pallas as pl
from jax.experimental.pallas import tpu as pltpu
from jax.sharding import PartitionSpec as P

HEAD_DIM = 64
EPS = 1e-05
BF = jnp.bfloat16
F32 = jnp.float32
ROOT_HALF = 0.7071067811865476
PHI_SCALE = 0.3989422804014327
VMEM_LIMIT = 60 * 1024 * 1024
TILE = 256


def mm(left, right):
    return lax.dot_general(left, right, (((1,), (0,)), ((), ())), preferred_element_type=F32)


def mm_rt(left, right):
    return lax.dot_general(left, right, (((1,), (1,)), ((), ())), preferred_element_type=F32)


def mm_lt(left, right):
    return lax.dot_general(left, right, (((0,), (0,)), ((), ())), preferred_element_type=F32)


def chip_grid(count):
    side = round((count / 2) ** (1 / 3))
    if 2 * side**3 == count:
        return (2 * side, side, side)
    return (count, 1, 1)


def shift(values, grid, axis, by):
    nz, ny, nx = grid
    pairs = []
    for z in range(nz):
        for y in range(ny):
            for x in range(nx):
                to = [z, y, x]
                to[axis] = (to[axis] + by) % grid[axis]
                pairs.append(((z * ny + y) * nx + x, (to[0] * ny + to[1]) * nx + to[2]))
    return lax.ppermute(values, "dp", pairs)


def swap_cores(values):
    size = lax.axis_size("head")
    return lax.ppermute(values, "head", [(i, (i + 1) % size) for i in range(size)])


def after(values, *earlier):
    return lax.optimization_barrier((values, *earlier))[0]


class Gathered:
    def __init__(self, grid, groups, places):
        self.grid = grid
        self.groups = groups
        self.places = places

    def wanted(self, keys):
        ids = []
        for key in keys:
            name = self.places[key][0]
            if name not in ids:
                ids.append(name)
        return ids

    def leaves(self, keys):
        return [leaf for name in self.wanted(keys) for leaf in jax.tree.leaves(self.groups[name])]

    def bind(self, keys, refs):
        bound, at = {}, 0
        for name in self.wanted(keys):
            leaves, tree = jax.tree.flatten(self.groups[name])
            bound[name] = jax.tree.unflatten(tree, refs[at : at + len(leaves)])
            at += len(leaves)
        return bound, refs[at:]

    def start(self, bound, key, dst, sem):
        name, items = self.places[key]
        if not isinstance(bound[name], list):
            ref = bound[name]
            for lane, width, row in items:
                pltpu.make_async_copy(
                    ref.at[:, pl.ds(lane, width)], dst.at[pl.ds(row, ref.shape[0]), :], sem
                ).start()
            return
        all_items = items
        nz, ny, nx = self.grid
        dp = lax.axis_index("dp")
        core = lax.axis_index("head")
        z, y, x = dp // (ny * nx), (dp // nx) % ny, dp % nx
        for at, half in enumerate(bound[name]):
            items = [item for item in all_items if item[0] == at]
            if not items:
                continue
            for last, pair in enumerate(half):
                for other in range(2):
                    ref = pair[other]
                    c = core if other == 0 else 1 - core
                    for first in range(ref.shape[0]):
                        for kz in range(nz):
                            zz = lax.rem(z + nz - kz, nz)
                            ky, kx = (first, last) if at == 0 else (last, first)
                            yy, xx = lax.rem(y + ny - ky, ny), lax.rem(x + nx - kx, nx)
                            owner = (zz * ny + yy) * nx + xx
                            for _, lane, width, place in items:
                                row, col = place(owner, c)
                                pltpu.make_async_copy(
                                    ref.at[first, kz, :, pl.ds(lane, width)],
                                    dst.at[pl.ds(row, ref.shape[2]), pl.ds(col, width)],
                                    sem,
                                ).start()


def wait_all(dst, sem):
    pltpu.make_async_copy(dst, dst, sem).wait()


def place_chip(rows, stride, base):
    def place(owner, c):
        return pl.multiple_of(owner * rows, 16), pl.multiple_of(c * stride + base, 128)

    return place


def place_core(rows, parts, part, base):
    def place(owner, c):
        return pl.multiple_of(((owner * 2 + c) * parts + part) * rows, 16), base

    return place


def tensor_items(name, rows, width, ff, parts):
    half = width // 2
    if name == "qkv":
        return [(half, lambda skip, i=i: place_chip(rows, half, i * width + skip)) for i in range(3)]
    if name == "out":
        return [(half, lambda skip: place_chip(rows, half, skip))]
    if name == "up":
        return [(ff // 2, lambda skip: place_chip(rows, ff // 2, skip))]
    return [(width, lambda skip, i=i: place_core(rows, parts, i, skip)) for i in range(parts)]


def cut_of(lanes):
    return (lanes // 2 + 127) // 128 * 128


def sds(shape, dtype):
    return jax.ShapeDtypeStruct(shape, dtype)


def kernel_call(body, outs, scratch, flops, scalars, blocks, raw, raw_outs=()):
    specs = [pl.BlockSpec(memory_space=pltpu.SMEM)] * len(scalars)
    specs += [pl.BlockSpec(memory_space=pltpu.VMEM)] * len(blocks)
    specs += [pl.BlockSpec(memory_space=pl.ANY)] * len(raw)
    moved = sum(v.size * v.dtype.itemsize for v in (*blocks, *raw, *outs))
    return pl.pallas_call(
        body,
        out_shape=tuple(outs),
        in_specs=specs,
        out_specs=tuple([pl.BlockSpec(memory_space=pltpu.VMEM)] * len(outs)),
        scratch_shapes=scratch,
        compiler_params=pltpu.CompilerParams(vmem_limit_bytes=VMEM_LIMIT),
        cost_estimate=pl.CostEstimate(flops=flops, bytes_accessed=moved, transcendentals=0),
    )(*scalars, *blocks, *raw)


def copy_in(src, dst, sem):
    pltpu.make_async_copy(src, dst, sem).start()


def mask_bias(len_ref, rows):
    length = len_ref[lax.axis_index("head")]
    near = lax.broadcasted_iota(jnp.int32, (rows, rows), 0) // length
    far = lax.broadcasted_iota(jnp.int32, (rows, rows), 1) // length
    return jnp.where(near == far, 0.0, -1e30).astype(F32)


def head_masks(rows):
    low = lax.broadcasted_iota(jnp.int32, (rows, 128), 1) < HEAD_DIM
    return low, jnp.zeros((rows, 128), BF)


def attend_forward(x, down, up, weights, layer, lengths):
    rows, width = x.shape
    keys = (("qkv", layer),)
    pairs = width // 128

    def body(len_ref, x_ref, down_ref, up_ref, *rest):
        bound, rest = weights.bind(keys, rest)
        q_ref, k_ref, v_ref, o_ref, lse_ref, mid_ref, w_ref, bias_ref, sem = rest
        weights.start(bound, keys[0], w_ref, sem)
        r = x_ref[...].astype(BF)
        mid = mm(r, down_ref[...]).astype(BF)
        mid_ref[...] = mid
        bias_ref[...] = mask_bias(len_ref, rows)
        wait_all(w_ref, sem)
        for at, out in enumerate((q_ref, k_ref, v_ref)):
            for j in range(0, width, TILE):
                c = at * width + j
                total = mm(r, w_ref[:, c : c + TILE])
                if at != 1:
                    total += mm(mid, up_ref[:, c : c + TILE])
                out[:, j : j + TILE] = total.astype(BF)
        low, zero = head_masks(rows)
        one_low = jnp.where(low, 1.0, 0.0).astype(BF)
        one_high = jnp.where(low, 0.0, 1.0).astype(BF)
        for p in range(pairs):
            lanes = slice(p * 128, p * 128 + 128)
            q2 = q_ref[:, lanes] * 0.125
            k2 = k_ref[:, lanes]
            v2 = v_ref[:, lanes]
            bias = bias_ref[...]
            s0 = mm_rt(q2, jnp.where(low, k2, zero)) + bias
            s1 = mm_rt(q2, jnp.where(low, zero, k2)) + bias
            m0 = jnp.max(s0, -1, keepdims=True)
            m1 = jnp.max(s1, -1, keepdims=True)
            e0 = jnp.exp(s0 - m0).astype(BF)
            e1 = jnp.exp(s1 - m1).astype(BF)
            v0 = jnp.concatenate([jnp.where(low, v2, zero), one_low], 1)
            v1 = jnp.concatenate([jnp.where(low, zero, v2), one_high], 1)
            both = mm(e0, v0) + mm(e1, v1)
            total = both[:, 128:]
            o_ref[:, lanes] = (both[:, :128] / total).astype(BF)
            flip = (jnp.where(low, m0, m1) + jnp.log(total)).T
            lse_ref[2 * p] = flip[0:8]
            lse_ref[2 * p + 1] = flip[64:72]

    act = sds((rows, width), BF)
    outs = (act, act, act, act, sds((2 * pairs, 8, rows), F32), sds((rows, 128), BF))
    return kernel_call(
        body,
        outs,
        [pltpu.VMEM((width, 3 * width), BF), pltpu.VMEM((rows, rows), F32), pltpu.SemaphoreType.DMA],
        6 * rows * width * width + 16 * rows * rows * width,
        (lengths,),
        (x, down, up),
        weights.leaves(keys),
    )


def normalize(values):
    center = values - jnp.mean(values, -1, keepdims=True)
    scale = lax.rsqrt(jnp.mean(center * center, -1, keepdims=True) + EPS)
    return center * scale, scale


def norm_backward(gn, n, scale):
    return (gn - jnp.mean(gn, -1, keepdims=True) - n * jnp.mean(gn * n, -1, keepdims=True)) * scale


def gelu_pair(u):
    below = 0.5 + 0.5 * lax.erf(u * ROOT_HALF)
    return u * below, below + u * (jnp.exp(-0.5 * (u * u)) * PHI_SCALE)


def dense_up(x, o_ref, wo_ref, wo_wait, wu_ref, wu_wait, gains, n1_ref, y_ref, yb_ref, slope_ref, a_ref):
    width, ff = wu_ref.shape
    wo_wait()
    for j in range(0, width, TILE):
        y_ref[:, j : j + TILE] = x(j) + mm(o_ref[...], wo_ref[:, j : j + TILE])
    n1, scale = normalize(y_ref[...])
    n1_ref[...] = n1.astype(BF)
    y = n1 * gains[0:1] + gains[1:2]
    y_ref[...] = y
    yb_ref[...] = y.astype(BF)
    wu_wait()
    for j in range(0, ff, TILE):
        value, slope = gelu_pair(mm(yb_ref[...], wu_ref[:, j : j + TILE]))
        slope_ref[:, j : j + TILE] = slope.astype(BF)
        a_ref[:, j : j + TILE] = value.astype(BF)
    return scale


def dense_forward(x, attended, rows8, weights, layer):
    rows, width = x.shape
    ff = weights.ff
    keys = (("out", layer), ("up", layer), ("down", layer))

    def body(x_ref, o_ref, rows_ref, *rest):
        bound, rest = weights.bind(keys, rest)
        n1_ref, rs_ref, slope_ref, out_ref, n2_ref, wo_ref, wu_ref, wd_ref, yb_ref, y_ref, a_ref, sem = rest
        for i, dst in enumerate((wo_ref, wu_ref, wd_ref)):
            weights.start(bound, keys[i], dst, sem.at[i])
        gains = rows_ref[...]
        rs1 = dense_up(
            lambda j: x_ref[:, j : j + TILE].astype(F32),
            o_ref,
            wo_ref,
            lambda: wait_all(wo_ref, sem.at[0]),
            wu_ref,
            lambda: wait_all(wu_ref, sem.at[1]),
            gains,
            n1_ref,
            y_ref,
            yb_ref,
            slope_ref,
            a_ref,
        )
        wait_all(wd_ref, sem.at[2])
        for j in range(0, width, TILE):
            y_ref[:, j : j + TILE] += mm(a_ref[...], wd_ref[:, j : j + TILE])
        n2, rs2 = normalize(y_ref[...])
        n2_ref[...] = n2.astype(BF)
        low = lax.broadcasted_iota(jnp.int32, (rows, 128), 1) < 64
        rs_ref[...] = jnp.where(low, rs1, rs2)
        out_ref[...] = n2 * gains[2:3] + gains[3:4]

    act, wide, hidden = sds((rows, width), BF), sds((rows, width), F32), sds((rows, ff), BF)
    return kernel_call(
        body,
        (act, sds((rows, 128), F32), hidden, wide, act),
        [
            pltpu.VMEM((width, width), BF),
            pltpu.VMEM((width, ff), BF),
            pltpu.VMEM((ff, width), BF),
            pltpu.VMEM((rows, width), BF),
            pltpu.VMEM((rows, width), F32),
            pltpu.VMEM((rows, ff), BF),
            pltpu.SemaphoreType.DMA((3,)),
        ],
        2 * rows * width * (width + 2 * ff),
        (),
        (x, attended, rows8),
        weights.leaves(keys),
    )


def attend_backward(q_ref, k_ref, v_ref, o_ref, go_ref, lse_ref, bias_ref, gq_ref, gk_ref, gv_ref):
    rows, width = q_ref.shape
    low, zero = head_masks(rows)
    for p in range(width // 128):
        lanes = slice(p * 128, p * 128 + 128)
        q2 = q_ref[:, lanes] * 0.125
        k2 = k_ref[:, lanes]
        v2 = v_ref[:, lanes]
        go2 = go_ref[:, lanes]
        flip = (go2.astype(F32) * o_ref[:, lanes].astype(F32)).T
        gq = gk = gv = None
        for h in range(2):
            keep = (lambda t: jnp.where(low, t, zero)) if h == 0 else (lambda t: jnp.where(low, zero, t))
            qh, kh, goh = keep(q2), keep(k2), keep(go2)
            dots = jnp.sum(flip[h * HEAD_DIM : (h + 1) * HEAD_DIM], 0, keepdims=True)
            prob = jnp.exp(mm_rt(k2, qh) + bias_ref[...] - lse_ref[2 * p + h][0:1])
            gs = (prob * (mm_rt(v2, goh) - dots)).astype(BF)
            to_q, to_k, to_v = mm_lt(gs, kh), mm(gs, qh), mm(prob.astype(BF), goh)
            gq = to_q if h == 0 else gq + to_q
            gk = to_k if h == 0 else gk + to_k
            gv = to_v if h == 0 else gv + to_v
        gq_ref[:, lanes] = (gq * 0.125).astype(BF)
        gk_ref[:, lanes] = gk.astype(BF)
        gv_ref[:, lanes] = gv.astype(BF)


def backward(saved, cotangent, rows8, downs, ups, weights, lengths):
    layers = len(saved)
    rows, width = cotangent.shape
    ff = weights.ff
    last = layers - 1
    keys = tuple((name, at) for at in reversed(range(layers)) for name in ("out", "up", "down", "qkv"))
    keys = keys[:-1]
    names = ("q", "k", "v", "o", "lse", "mid")
    early = ("n1", "rs", "slope", "n2", "r")
    raw = [cotangent, saved[last]["x"]]
    for at in reversed(range(layers)):
        raw += [saved[at][name] for name in names + (early if at < last else ())]

    def body(len_ref, rows_ref, down_ref, up_ref, *rest):
        cot_in, x_in = rest[:2]
        rest = rest[2:]
        given = [None] * layers
        for at in reversed(range(layers)):
            here = names + (early if at < last else ())
            given[at] = dict(zip(here, rest))
            rest = rest[len(here) :]
        bound, rest = weights.bind(keys, rest)
        out_ref, sums_ref, ghid_ref, gq_ref, gk_ref, gv_ref, gm_ref = rest[:7]
        (wd_ref, wu_ref, wo_ref, wq_ref, cot_ref, g_ref, a_ref, wide_ref, gb_ref, go_ref, bias_ref) = rest[7:18]
        keep = dict(zip(names + early, rest[18:29]))
        sem = rest[29]
        sems = {n: sem.at[i] for i, n in enumerate(names + early + ("down", "up", "out", "qkv", "cot", "x"))}

        def fetch(at, *which):
            for name in which:
                copy_in(given[at][name], keep[name], sems[name])

        def take(*which):
            for name in which:
                wait_all(keep[name], sems[name])

        copy_in(x_in, g_ref, sems["x"])
        fetch(last, "o")
        weights.start(bound, ("out", last), wo_ref, sems["out"])
        weights.start(bound, ("up", last), wu_ref, sems["up"])
        weights.start(bound, ("down", last), wd_ref, sems["down"])
        copy_in(cot_in, cot_ref, sems["cot"])
        fetch(last, "q", "k", "v", "lse", "mid")
        weights.start(bound, ("qkv", last), wq_ref, sems["qkv"])
        bias_ref[...] = mask_bias(len_ref, rows)
        for at in reversed(range(layers)):
            gains = rows_ref[8 * at : 8 * at + 8]
            if at == last:
                wait_all(g_ref, sems["x"])
                take("o")
                keep["r"][...] = g_ref[...].astype(BF)
                scale1 = dense_up(
                    lambda j: g_ref[:, j : j + TILE],
                    keep["o"],
                    wo_ref,
                    lambda: wait_all(wo_ref, sems["out"]),
                    wu_ref,
                    lambda: wait_all(wu_ref, sems["up"]),
                    gains,
                    keep["n1"],
                    wide_ref,
                    gb_ref,
                    keep["slope"],
                    a_ref,
                )
                keep["rs"][...] = jnp.broadcast_to(scale1, (rows, 128))
                wait_all(wd_ref, sems["down"])
                for j in range(0, width, TILE):
                    wide_ref[:, j : j + TILE] += mm(a_ref[...], wd_ref[:, j : j + TILE])
                n2, scale2 = normalize(wide_ref[...])
                out_ref[...] = (n2 * gains[2:3] + gains[3:4]).astype(out_ref.dtype)
                wait_all(cot_ref, sems["cot"])
                incoming = cot_ref[...].astype(F32)
            else:
                take("rs", "n2")
                n2, scale2 = keep["n2"][...].astype(F32), keep["rs"][:, 64:65]
                incoming = g_ref[...]
                wait_all(wd_ref, sems["down"])
                wait_all(wu_ref, sems["up"])
                wait_all(wo_ref, sems["out"])
                take("slope", "n1")
            gz = norm_backward(incoming * gains[2:3], n2, scale2)
            wide_ref[...] = gz
            gb_ref[...] = gz.astype(BF)
            for j in range(0, ff, TILE):
                ga = mm_rt(gb_ref[...], wd_ref[j : j + TILE, :])
                a_ref[:, j : j + TILE] = (ga * keep["slope"][:, j : j + TILE].astype(F32)).astype(BF)
            for j in range(0, width, TILE):
                wide_ref[:, j : j + TILE] += mm_rt(a_ref[...], wu_ref[j : j + TILE, :])
            scale1 = keep["rs"][:, 0:1]
            ghid = norm_backward(wide_ref[...] * gains[0:1], keep["n1"][...].astype(F32), scale1)
            ghid_ref[...] = ghid
            gb_ref[...] = ghid.astype(BF)
            for j in range(0, width, TILE):
                go_ref[:, j : j + TILE] = mm_rt(gb_ref[...], wo_ref[j : j + TILE, :]).astype(BF)
            if at > 0:
                weights.start(bound, ("down", at - 1), wd_ref, sems["down"])
                fetch(at - 1, "n2", "rs", "slope", "n1")
                weights.start(bound, ("up", at - 1), wu_ref, sems["up"])
                weights.start(bound, ("out", at - 1), wo_ref, sems["out"])
            take("q", "k", "v", "lse", *(() if at == last else ("o",)))
            attend_backward(
                keep["q"], keep["k"], keep["v"], keep["o"], go_ref, keep["lse"], bias_ref, gq_ref, gk_ref, gv_ref
            )
            if at > 0:
                fetch(at - 1, "q", "k", "v", "o", "lse")
            up = up_ref.at[at]
            gm = mm_rt(gq_ref[...], up[:, :width]) + mm_rt(gv_ref[...], up[:, 2 * width :])
            gm = gm.astype(BF)
            take("mid", *(() if at == last else ("r",)))
            base = 32 * at
            sums_ref[base : base + 16] = mm_lt(gm, keep["r"][...])[0:16]
            sums_ref[base + 16 : base + 24] = 2.0 * mm_lt(keep["mid"][...], gq_ref[...])[0:8]
            sums_ref[base + 24 : base + 32] = 2.0 * mm_lt(keep["mid"][...], gv_ref[...])[8:16]
            if at == 0:
                gm_ref[...] = gm
                continue
            fetch(at - 1, "mid", "r")
            wait_all(wq_ref, sems["qkv"])
            for j in range(0, width, TILE):
                rs = slice(j, j + TILE)
                total = ghid_ref[:, rs] + mm_rt(gm, down_ref[at, rs, :])
                total += mm_rt(gq_ref[...], wq_ref[rs, :width])
                total += mm_rt(gk_ref[...], wq_ref[rs, width : 2 * width])
                total += mm_rt(gv_ref[...], wq_ref[rs, 2 * width :])
                g_ref[:, rs] = total
            if at > 1:
                weights.start(bound, ("qkv", at - 1), wq_ref, sems["qkv"])

    act = sds((rows, width), BF)
    outs = (act, sds((32 * layers, width), F32), sds((rows, width), F32), act, act, act, sds((rows, 128), BF))
    scratch = [
        pltpu.VMEM((ff, width), BF),
        pltpu.VMEM((width, ff), BF),
        pltpu.VMEM((width, width), BF),
        pltpu.VMEM((width, 3 * width), BF),
        pltpu.VMEM((rows, width), cotangent.dtype),
        pltpu.VMEM((rows, width), F32),
        pltpu.VMEM((rows, ff), BF),
        pltpu.VMEM((rows, width), F32),
        pltpu.VMEM((rows, width), BF),
        pltpu.VMEM((rows, width), BF),
        pltpu.VMEM((rows, rows), F32),
    ]
    like = {**saved[last], **saved[0]}
    scratch += [pltpu.VMEM(like[name].shape, like[name].dtype) for name in names + early]
    scratch += [pltpu.SemaphoreType.DMA((len(names) + len(early) + 6,))]
    return kernel_call(
        body,
        outs,
        scratch,
        layers * (6 * rows * width * (2 * width + ff) + 40 * rows * rows * width),
        (lengths,),
        (rows8, downs, ups),
        raw + weights.leaves(keys),
    )


def input_grad(ghid, gq, gk, gv, gm, down, weights):
    rows, width = ghid.shape
    keys = (("qkv", 0),)

    def body(ghid_ref, gq_ref, gk_ref, gv_ref, gm_ref, down_ref, *rest):
        bound, rest = weights.bind(keys, rest)
        out_ref, w_ref, sem = rest
        weights.start(bound, keys[0], w_ref, sem)
        wait_all(w_ref, sem)
        for j in range(0, width, TILE):
            rs = slice(j, j + TILE)
            total = ghid_ref[:, rs] + mm_rt(gm_ref[...], down_ref[rs, :])
            total += mm_rt(gq_ref[...], w_ref[rs, :width])
            total += mm_rt(gk_ref[...], w_ref[rs, width : 2 * width])
            total += mm_rt(gv_ref[...], w_ref[rs, 2 * width :])
            out_ref[:, rs] = total

    return kernel_call(
        body,
        (sds((rows, width), F32),),
        [pltpu.VMEM((width, 3 * width), BF), pltpu.SemaphoreType.DMA],
        6 * rows * width * width,
        (),
        (ghid, gq, gk, gv, gm, down),
        weights.leaves(keys),
    )[0]


def whole_weights(grid, tensors):
    w_query, w_key, w_value, w_out, w_up, w_down = tensors
    groups, places = {}, {}
    half = w_query.shape[2]
    for at in range(w_query.shape[0]):
        qkv = jnp.concatenate([w[at].astype(BF) for w in (w_query, w_key, w_value)], 1)
        qkv = lax.all_gather(qkv, "dp", axis=0, tiled=True)
        qkv = lax.all_gather(qkv, "head", axis=0, tiled=False)
        heads, width = qkv.shape[0], qkv.shape[1]
        qkv = qkv.reshape(heads, width, 3, half).transpose(1, 2, 0, 3).reshape(width, 3 * heads * half)
        groups["qkv", at] = qkv
        for name, w in (("out", w_out), ("up", w_up), ("down", w_down)):
            groups[name, at] = lax.all_gather(w[at].astype(BF), ("dp", "head"), axis=0, tiled=True)
        for name in ("qkv", "out", "up", "down"):
            places[name, at] = ((name, at), [(0, groups[name, at].shape[1], 0)])
    return Gathered(grid, groups, places)


class Chunk:
    def __init__(self, packed, grid):
        self.grid = grid
        self.packed = packed
        self.cut = cut_of(packed.shape[1])

    def spread_z(self, *gates):
        packed = after(self.packed, *gates) if gates else self.packed
        self.line = [packed] + [shift(packed, self.grid, 0, k) for k in range(1, self.grid[0])]
        return self.line[1:]

    def spread_first(self, *gates):
        line = lax.optimization_barrier((*self.line, *gates))[: len(self.line)]
        parts = (jnp.stack([t[:, : self.cut] for t in line]), jnp.stack([t[:, self.cut :] for t in line]))
        self.first = []
        come = []
        for part, axis in zip(parts, (1, 2)):
            moved = [shift(part, self.grid, axis, k) for k in range(1, self.grid[axis])]
            come += moved
            self.first.append([part] + moved)
        return come

    def spread_second(self, *gates):
        split = len(self.first[0])
        flat = (*self.first[0], *self.first[1])
        flat = lax.optimization_barrier((*flat, *gates))[: len(flat)]
        lines = [jnp.stack(flat[:split]), jnp.stack(flat[split:])]
        self.halves = []
        come = []
        for line, axis in zip(lines, (2, 1)):
            moved = [shift(line, self.grid, axis, k) for k in range(1, self.grid[axis])]
            come += moved
            self.halves.append([line] + moved)
        return come

    def swap(self, *gates):
        if gates:
            leaves, tree = jax.tree.flatten(self.halves)
            leaves = lax.optimization_barrier((*leaves, *gates))[: len(leaves)]
            self.halves = jax.tree.unflatten(tree, leaves)
        return [[(own, swap_cores(own)) for own in half] for half in self.halves]


def gather_and_run(chunks, weights, tokens, attention, dense):
    def arrive(index, *gates):
        weights.groups[index] = c[index].swap(*gates)

    c = chunks
    z0 = c[0].spread_z()
    c[1].spread_z()
    first0 = c[0].spread_first()
    c[2].spread_z(*z0, c[1].packed)
    second0 = c[0].spread_second()
    first1 = c[1].spread_first(*second0)
    arrive(0)
    o = attention(0, tokens)
    second1 = c[1].spread_second()
    first2 = c[2].spread_first(*first1, o)
    c[2].spread_second(*second1)
    arrive(1)
    arrive(2)
    attention(1, dense(0, tokens, o))


def sum_over_devices(sums, grid):
    half = sums.shape[1] // 2
    core = lax.axis_index("head")
    mine = lax.dynamic_slice_in_dim(sums, core * half, half, 1)
    other = lax.dynamic_slice_in_dim(sums, (1 - core) * half, half, 1)
    total = mine + swap_cores(other)
    for axis in (2, 1, 0):
        parts = [total] + [shift(total, grid, axis, k) for k in range(1, grid[axis])]
        total = functools.reduce(jnp.add, parts)
    return total


def pack_chunks(tensors):
    w_query, w_key, w_value, w_out, w_up, w_down = tensors
    layers, rows, half = w_query.shape
    width, ff = 2 * half, w_up.shape[2]
    core = lax.axis_index("head")
    both = jnp.concatenate([w_out[0], w_up[0]], 1).astype(BF)

    def columns(which):
        return jnp.concatenate(
            [
                lax.dynamic_slice_in_dim(both, which * half, half, 1),
                lax.dynamic_slice_in_dim(both, width + which * (ff // 2), ff // 2, 1),
            ],
            1,
        )

    mine, come = columns(core), swap_cores(columns(1 - core))
    both = jnp.concatenate([jnp.where(core == 0, mine, come), jnp.where(core == 0, come, mine)], 0)
    parts = w_down.shape[1] // rows
    made = {("qkv", at): [w[at].astype(BF) for w in (w_query, w_key, w_value)] for at in range(layers)}
    made["out", 0] = [both[:, :half]]
    made["up", 0] = [both[:, half:]]
    made["down", 0] = [w_down[0, i * rows : (i + 1) * rows].astype(BF) for i in range(parts)]
    chunks = [[("qkv", 0)], [("out", 0), ("up", 0)], [("down", 0), ("qkv", 1)]]
    packs, places = [], {}
    for index, keys in enumerate(chunks):
        lanes = sum(block.shape[1] for key in keys for block in made[key])
        cut, at = cut_of(lanes), 0
        for key in keys:
            items = []
            for wide, placer in tensor_items(key[0], rows, width, ff, parts):
                for half_at, low, high in ((0, 0, cut), (1, cut, lanes)):
                    start, stop = max(at, low), min(at + wide, high)
                    if start < stop:
                        items.append((half_at, start - low, stop - start, placer(start - at)))
                at += wide
            places[key] = (index, items)
        packs.append(jnp.concatenate([block for key in keys for block in made[key]], 1))
    return packs, places


def gather_dense(w_out, w_up, w_down):
    rows, ff = w_up.shape
    width = w_out.shape[1]
    parts = w_down.shape[0] // rows
    up = w_up.astype(BF).reshape(rows, ff // (parts * rows), parts, rows).swapaxes(1, 2).reshape(rows, ff)
    blocks = [w_down[i * rows : (i + 1) * rows].astype(BF) for i in range(parts)]
    packed = jnp.concatenate([w_out.astype(BF), up, *blocks], 1)
    whole = lax.all_gather(packed, ("dp", "head"), axis=0, tiled=True)
    places = {
        "out": [(0, width, 0)],
        "up": [(width, ff, 0)],
        "down": [(width + ff + i * width, width, i * width) for i in range(parts)],
    }
    return whole, places


def body(
    tokens,
    seq_len,
    w_query,
    w_key,
    w_value,
    w_out,
    w_up,
    w_down,
    a_query,
    b_query,
    a_value,
    b_value,
    ln_gain,
    ln_bias,
    cotangent,
):
    layers, width = w_query.shape[0], tokens.shape[1]
    rank = a_query.shape[2]
    half = b_query.shape[2]
    grid = chip_grid(lax.axis_size("dp"))
    core = lax.axis_index("head")
    tensors = (w_query, w_key, w_value, w_out, w_up, w_down)

    own = jnp.stack([b_query, b_value], 1).astype(BF)
    other = swap_cores(own)
    up_all = jnp.concatenate([jnp.where(core == 0, own, other), jnp.where(core == 0, other, own)], -1)
    pair = jnp.concatenate([a_query, a_value], 2).astype(BF)
    downs = jnp.pad(pair, ((0, 0), (0, 0), (0, 128 - 2 * rank)))
    q_up = jnp.pad(2.0 * up_all[:, 0], ((0, 0), (0, 128 - rank), (0, 0)))
    v_up = jnp.pad(2.0 * up_all[:, 1], ((0, 0), (rank, 128 - 2 * rank), (0, 0)))
    ups = jnp.concatenate([q_up, jnp.zeros_like(q_up), v_up], 2)
    gains = jnp.stack([ln_gain[:, 0], ln_bias[:, 0], ln_gain[:, 1], ln_bias[:, 1]], 1)
    rows8 = jnp.pad(gains, ((0, 0), (0, 4), (0, 0)))

    pieces = w_query.shape[1] % 16 == 0 and lax.axis_size("head") == 2 and layers == 2
    saved = []
    if not pieces:
        weights = whole_weights(grid, tensors)
        weights.ff = w_up.shape[2]
    else:
        whole, whole_places = gather_dense(w_out[1], w_up[1], w_down[1])
        packs, places = pack_chunks(tensors)
        for name, lanes in whole_places.items():
            places[name, 1] = ("dense", lanes)
        chunks = [Chunk(packed, grid) for packed in packs]
        weights = Gathered(grid, {"dense": whole}, places)
        weights.ff = w_up.shape[2]

    def attention(at, stream):
        q, k, v, o, lse, mid = attend_forward(stream, downs[at], ups[at], weights, at, seq_len)
        saved.append({"q": q, "k": k, "v": v, "o": o, "lse": lse, "mid": mid, "x": stream})
        return o

    def dense(at, stream, attended):
        got = dense_forward(stream, attended, rows8[at], weights, at)
        saved[at].update(zip(("n1", "rs", "slope", "out", "n2"), got))
        saved[at]["r"] = stream.astype(BF)
        return saved[at]["out"]

    if not pieces:
        stream = tokens
        for at in range(layers):
            attended = attention(at, stream)
            if at < layers - 1:
                stream = dense(at, stream, attended)
    else:
        gather_and_run(chunks, weights, tokens, attention, dense)
    output, sums, ghid, gq, gk, gv, gm = backward(
        saved, cotangent, rows8.reshape(8 * layers, width), downs, ups, weights, seq_len
    )
    grad = input_grad(ghid, gq, gk, gv, gm, downs[0], weights)
    total = sum_over_devices(sums, grid).reshape(layers, 4, rank, half)
    lower = total[:, :2].reshape(layers * 2 * rank, half)
    far = swap_cores(lower)
    lower = jnp.concatenate([jnp.where(core == 0, lower, far), jnp.where(core == 0, far, lower)], 1)
    lower = lower.reshape(layers, 2, rank, width).transpose(0, 1, 3, 2)
    return (output, grad, lower[:, 0], total[:, 2], lower[:, 1], total[:, 3])


def solution(mesh):
    both = ("dp", "head")
    placed = (
        P(both, None),
        P("dp"),
        P(None, "dp", "head"),
        P(None, "dp", "head"),
        P(None, "dp", "head"),
        P(None, both, None),
        P(None, both, None),
        P(None, both, None),
        P(),
        P(None, None, "head"),
        P(),
        P(None, None, "head"),
        P(),
        P(),
        P(both, None),
    )
    return jax.shard_map(
        body,
        mesh=mesh,
        in_specs=placed,
        out_specs=(
            P(both, None),
            P(both, None),
            P(),
            P(None, None, "head"),
            P(),
            P(None, None, "head"),
        ),
        check_vma=False,
    )
```

```python
import functools
import itertools

import jax
import jax.numpy as jnp
from jax import lax
from jax.experimental import pallas as pl
from jax.experimental.pallas import tpu as pltpu
from jax.sharding import PartitionSpec as P

HEAD_DIM = 64
EPS = 1e-05
BF = jnp.bfloat16
F32 = jnp.float32
ROOT_HALF = 0.7071067811865476
PHI_SCALE = 0.3989422804014327
VMEM_LIMIT = 60 * 1024 * 1024
TILE = 256


def mm(left, right):
    return lax.dot_general(left, right, (((1,), (0,)), ((), ())), preferred_element_type=F32)


def mm_rt(left, right):
    return lax.dot_general(left, right, (((1,), (1,)), ((), ())), preferred_element_type=F32)


def mm_lt(left, right):
    return lax.dot_general(left, right, (((0,), (0,)), ((), ())), preferred_element_type=F32)


def chip_grid(count):
    side = round((count / 2) ** (1 / 3))
    if 2 * side**3 == count:
        return (2 * side, side, side)
    return (count, 1, 1)


def shift(values, grid, axis, by):
    return move(values, grid, [by if i == axis else 0 for i in range(3)])


def move(values, grid, by):
    nz, ny, nx = grid
    pairs = []
    for z in range(nz):
        for y in range(ny):
            for x in range(nx):
                to = [(at + step) % size for at, step, size in zip((z, y, x), by, grid)]
                pairs.append(((z * ny + y) * nx + x, (to[0] * ny + to[1]) * nx + to[2]))
    return lax.ppermute(values, "dp", pairs)


def swap_cores(values):
    size = lax.axis_size("head")
    return lax.ppermute(values, "head", [(i, (i + 1) % size) for i in range(size)])


def after(values, *earlier):
    return lax.optimization_barrier((values, *earlier))[0]


class Gathered:
    def __init__(self, grid, groups, places):
        self.grid = grid
        self.groups = groups
        self.places = places

    def wanted(self, keys):
        ids = []
        for key in keys:
            name = self.places[key][0]
            if name not in ids:
                ids.append(name)
        return ids

    def leaves(self, keys):
        return [leaf for name in self.wanted(keys) for leaf in jax.tree.leaves(self.groups[name])]

    def bind(self, keys, refs):
        bound, at = {}, 0
        for name in self.wanted(keys):
            leaves, tree = jax.tree.flatten(self.groups[name])
            bound[name] = jax.tree.unflatten(tree, refs[at : at + len(leaves)])
            at += len(leaves)
        return bound, refs[at:]

    def start(self, bound, key, dst, sems):
        name, items = self.places[key]
        if not isinstance(bound[name], list):
            run = dst.shape[1] // len(sems)
            for i, sem in enumerate(sems):
                lanes = pl.ds(i * run, run)
                pltpu.make_async_copy(bound[name].at[:, lanes], dst.at[:, lanes], sem).start()
            return
        nz, ny, nx = self.grid
        dp = lax.axis_index("dp")
        core = lax.axis_index("head")
        z, y, x = dp // (ny * nx), (dp // nx) % ny, dp % nx
        runs = range(len(sems)) if len(sems) > 1 else (None,)
        for wanted, (at, half) in itertools.product(runs, enumerate(bound[name])):
            here = [item for item in items if item[0] == at and wanted in (None, item[4])]
            if not here:
                continue
            for last, pair in enumerate(half):
                for other in range(2):
                    ref = pair[other]
                    c = core if other == 0 else 1 - core
                    for first in range(ref.shape[0]):
                        for kz in range(nz):
                            zz = lax.rem(z + nz - kz, nz)
                            ky, kx = (first, last) if at == 0 else (last, first)
                            yy, xx = lax.rem(y + ny - ky, ny), lax.rem(x + nx - kx, nx)
                            owner = (zz * ny + yy) * nx + xx
                            for _, lane, width, place, run in here:
                                row, col = place(owner, c)
                                pltpu.make_async_copy(
                                    ref.at[first, kz, :, pl.ds(lane, width)],
                                    dst.at[pl.ds(row, ref.shape[2]), pl.ds(col, width)],
                                    sems[run if len(sems) > 1 else 0],
                                ).start()


def wait_all(dst, sem):
    pltpu.make_async_copy(dst, dst, sem).wait()


def place_chip(rows, stride, base):
    def place(owner, c):
        return pl.multiple_of(owner * rows, 16), pl.multiple_of(c * stride + base, 128)

    return place


def place_core(rows, parts, part, base):
    def place(owner, c):
        return pl.multiple_of(((owner * 2 + c) * parts + part) * rows, 16), base

    return place


def tensor_items(name, rows, width, ff, parts):
    half = width // 2
    if name == "qkv":
        return [(half, lambda skip, i=i: place_chip(rows, half, i * width + skip)) for i in range(3)]
    if name == "out":
        return [(half, lambda skip: place_chip(rows, half, skip))]
    if name == "up":
        return [(ff // 2, lambda skip: place_chip(rows, ff // 2, skip))]
    return [(width, lambda skip, i=i: place_core(rows, parts, i, skip)) for i in range(parts)]


def cut_of(lanes):
    return (lanes // 2 + 127) // 128 * 128


def sds(shape, dtype):
    return jax.ShapeDtypeStruct(shape, dtype)


def kernel_call(body, outs, scratch, flops, scalars, blocks, raw, raw_outs=0):
    specs = [pl.BlockSpec(memory_space=pltpu.SMEM)] * len(scalars)
    specs += [pl.BlockSpec(memory_space=pltpu.VMEM)] * len(blocks)
    specs += [pl.BlockSpec(memory_space=pl.ANY)] * len(raw)
    moved = sum(v.size * v.dtype.itemsize for v in (*blocks, *raw, *outs))
    return pl.pallas_call(
        body,
        out_shape=tuple(outs),
        in_specs=specs,
        out_specs=tuple(
            pl.BlockSpec(memory_space=pl.ANY if i < raw_outs else pltpu.VMEM) for i in range(len(outs))
        ),
        scratch_shapes=scratch,
        compiler_params=pltpu.CompilerParams(vmem_limit_bytes=VMEM_LIMIT),
        cost_estimate=pl.CostEstimate(flops=flops, bytes_accessed=moved, transcendentals=0),
    )(*scalars, *blocks, *raw)


def copy_in(src, dst, sem):
    pltpu.make_async_copy(src, dst, sem).start()


def mask_bias(len_ref, rows):
    length = len_ref[lax.axis_index("head")]
    near = lax.broadcasted_iota(jnp.int32, (rows, rows), 0) // length
    far = lax.broadcasted_iota(jnp.int32, (rows, rows), 1) // length
    return jnp.where(near == far, 0.0, -1e30).astype(F32)


def head_masks(rows):
    low = lax.broadcasted_iota(jnp.int32, (rows, 128), 1) < HEAD_DIM
    return low, jnp.zeros((rows, 128), BF)


def project(r, down, up_ref, w_ref, w_wait, mid_ref, outs, done):
    width = w_ref.shape[0]
    mid = mm(r, down).astype(BF)
    mid_ref[...] = mid
    for at in range(3):
        w_wait(at)
        for j in range(0, width, TILE):
            c = at * width + j
            total = mm(r, w_ref[:, c : c + TILE])
            if at != 1:
                total += mm(mid, up_ref(slice(c, c + TILE)))
            outs[at][:, j : j + TILE] = total.astype(BF)
        done(at)


def attend(q_ref, k_ref, v_ref, o_ref, lse_ref, bias_ref):
    rows, width = q_ref.shape
    low, zero = head_masks(rows)
    one_low = jnp.where(low, 1.0, 0.0).astype(BF)
    one_high = jnp.where(low, 0.0, 1.0).astype(BF)
    for p in range(width // 128):
        lanes = slice(p * 128, p * 128 + 128)
        q2 = q_ref[:, lanes] * 0.125
        k2 = k_ref[:, lanes]
        v2 = v_ref[:, lanes]
        bias = bias_ref[...]
        s0 = mm_rt(q2, jnp.where(low, k2, zero)) + bias
        s1 = mm_rt(q2, jnp.where(low, zero, k2)) + bias
        m0 = jnp.max(s0, -1, keepdims=True)
        m1 = jnp.max(s1, -1, keepdims=True)
        e0 = jnp.exp(s0 - m0).astype(BF)
        e1 = jnp.exp(s1 - m1).astype(BF)
        v0 = jnp.concatenate([jnp.where(low, v2, zero), one_low], 1)
        v1 = jnp.concatenate([jnp.where(low, zero, v2), one_high], 1)
        both = mm(e0, v0) + mm(e1, v1)
        total = both[:, 128:]
        o_ref[:, lanes] = (both[:, :128] / total).astype(BF)
        flip = (jnp.where(low, m0, m1) + jnp.log(total)).T
        lse_ref[2 * p] = flip[0:8]
        lse_ref[2 * p + 1] = flip[64:72]


def third(ref, at):
    width = ref.shape[0]
    return ref.at[:, pl.ds(at * width, width)]


def project_forward(x, down, up, weights, layer):
    rows, width = x.shape
    keys = (("qkv", layer),)

    def body(x_in, down_in, up_in, *rest):
        bound, rest = weights.bind(keys, rest)
        far, mid_ref, near = rest[:3], rest[3], rest[4:7]
        w_ref, x_ref, down_ref, up_ref, sem, sem_out = rest[7:]

        def give(at, op="start"):
            getattr(pltpu.make_async_copy(near[at], far[at], sem_out.at[at]), op)()

        copy_in(x_in, x_ref, sem.at[3])
        copy_in(down_in, down_ref, sem.at[4])
        copy_in(up_in, up_ref, sem.at[5])
        weights.start(bound, keys[0], w_ref, [sem.at[at] for at in range(3)])
        for ref, at in ((x_ref, 3), (down_ref, 4), (up_ref, 5)):
            wait_all(ref, sem.at[at])
        project(
            x_ref[...].astype(BF),
            down_ref[...],
            lambda columns: up_ref[:, columns],
            w_ref,
            lambda at: wait_all(third(w_ref, at), sem.at[at]),
            mid_ref,
            near,
            give,
        )
        for at in range(3):
            give(at, "wait")

    act = sds((rows, width), BF)
    return kernel_call(
        body,
        (act, act, act, sds((rows, 128), BF)),
        [pltpu.VMEM((rows, width), BF)] * 3
        + [
            pltpu.VMEM((width, 3 * width), BF),
            pltpu.VMEM(x.shape, x.dtype),
            pltpu.VMEM(down.shape, BF),
            pltpu.VMEM(up.shape, BF),
            pltpu.SemaphoreType.DMA((6,)),
            pltpu.SemaphoreType.DMA((3,)),
        ],
        6 * rows * width * width,
        (),
        (),
        [x, down, up] + weights.leaves(keys),
        raw_outs=3,
    )


def attend_forward(q, k, v, lengths):
    rows, width = q.shape

    def body(len_ref, q_ref, k_ref, v_ref, o_ref, lse_ref, bias_ref):
        bias_ref[...] = mask_bias(len_ref, rows)
        attend(q_ref, k_ref, v_ref, o_ref, lse_ref, bias_ref)

    return kernel_call(
        body,
        (sds((rows, width), BF), sds((width // HEAD_DIM, 8, rows), F32)),
        [pltpu.VMEM((rows, rows), F32)],
        16 * rows * rows * width,
        (lengths,),
        (q, k, v),
        [],
    )


def normalize(values):
    center = values - jnp.mean(values, -1, keepdims=True)
    scale = lax.rsqrt(jnp.mean(center * center, -1, keepdims=True) + EPS)
    return center * scale, scale


def norm_backward(gn, n, scale):
    return (gn - jnp.mean(gn, -1, keepdims=True) - n * jnp.mean(gn * n, -1, keepdims=True)) * scale


def gelu_pair(u):
    below = 0.5 + 0.5 * lax.erf(u * ROOT_HALF)
    return u * below, below + u * (jnp.exp(-0.5 * (u * u)) * PHI_SCALE)


def dense_up(x, o_ref, wo_ref, wo_wait, wu_ref, wu_wait, gains, n1_ref, y_ref, yb_ref, slope_ref, a_ref):
    width, ff = wu_ref.shape
    wo_wait()
    for j in range(0, width, TILE):
        y_ref[:, j : j + TILE] = x(j) + mm(o_ref[...], wo_ref[:, j : j + TILE])
    n1, scale = normalize(y_ref[...])
    n1_ref[...] = n1.astype(BF)
    y = n1 * gains[0:1] + gains[1:2]
    y_ref[...] = y
    yb_ref[...] = y.astype(BF)
    for j in range(0, ff, TILE):
        wu_wait(j)
        value, slope = gelu_pair(mm(yb_ref[...], wu_ref[:, j : j + TILE]))
        slope_ref[:, j : j + TILE] = slope.astype(BF)
        a_ref[:, j : j + TILE] = value.astype(BF)
    return scale


def dense_forward(x, attended, rows8, weights, layer):
    rows, width = x.shape
    ff = weights.ff
    keys = (("out", layer), ("up", layer), ("down", layer))

    def body(x_ref, o_ref, rows_ref, *rest):
        bound, rest = weights.bind(keys, rest)
        n1_ref, rs_ref, slope_ref, out_ref, n2_ref, wo_ref, wu_ref, wd_ref, yb_ref, y_ref, a_ref, sem = rest
        for i, dst in enumerate((wo_ref, wu_ref, wd_ref)):
            weights.start(bound, keys[i], dst, [sem.at[i]])
        gains = rows_ref[...]
        rs1 = dense_up(
            lambda j: x_ref[:, j : j + TILE].astype(F32),
            o_ref,
            wo_ref,
            lambda: wait_all(wo_ref, sem.at[0]),
            wu_ref,
            lambda j: wait_all(wu_ref, sem.at[1]) if j == 0 else None,
            gains,
            n1_ref,
            y_ref,
            yb_ref,
            slope_ref,
            a_ref,
        )
        wait_all(wd_ref, sem.at[2])
        for j in range(0, width, TILE):
            y_ref[:, j : j + TILE] += mm(a_ref[...], wd_ref[:, j : j + TILE])
        n2, rs2 = normalize(y_ref[...])
        n2_ref[...] = n2.astype(BF)
        low = lax.broadcasted_iota(jnp.int32, (rows, 128), 1) < 64
        rs_ref[...] = jnp.where(low, rs1, rs2)
        out_ref[...] = n2 * gains[2:3] + gains[3:4]

    act, wide, hidden = sds((rows, width), BF), sds((rows, width), F32), sds((rows, ff), BF)
    return kernel_call(
        body,
        (act, sds((rows, 128), F32), hidden, wide, act),
        [
            pltpu.VMEM((width, width), BF),
            pltpu.VMEM((width, ff), BF),
            pltpu.VMEM((ff, width), BF),
            pltpu.VMEM((rows, width), BF),
            pltpu.VMEM((rows, width), F32),
            pltpu.VMEM((rows, ff), BF),
            pltpu.SemaphoreType.DMA((3,)),
        ],
        2 * rows * width * (width + 2 * ff),
        (),
        (x, attended, rows8),
        weights.leaves(keys),
    )


def attend_backward(q_ref, k_ref, v_ref, o_ref, go_ref, lse_ref, bias_ref, gq_ref, gk_ref, gv_ref):
    rows, width = q_ref.shape
    low, zero = head_masks(rows)
    for p in range(width // 128):
        lanes = slice(p * 128, p * 128 + 128)
        q2 = q_ref[:, lanes] * 0.125
        k2 = k_ref[:, lanes]
        v2 = v_ref[:, lanes]
        go2 = go_ref[:, lanes]
        flip = (go2.astype(F32) * o_ref[:, lanes].astype(F32)).T
        gq = gk = gv = None
        for h in range(2):
            keep = (lambda t: jnp.where(low, t, zero)) if h == 0 else (lambda t: jnp.where(low, zero, t))
            qh, kh, goh = keep(q2), keep(k2), keep(go2)
            dots = jnp.sum(flip[h * HEAD_DIM : (h + 1) * HEAD_DIM], 0, keepdims=True)
            prob = jnp.exp(mm_rt(k2, qh) + bias_ref[...] - lse_ref[2 * p + h][0:1])
            gs = (prob * (mm_rt(v2, goh) - dots)).astype(BF)
            to_q, to_k, to_v = mm_lt(gs, kh), mm(gs, qh), mm(prob.astype(BF), goh)
            gq = to_q if h == 0 else gq + to_q
            gk = to_k if h == 0 else gk + to_k
            gv = to_v if h == 0 else gv + to_v
        gq_ref[:, lanes] = (gq * 0.125).astype(BF)
        gk_ref[:, lanes] = gk.astype(BF)
        gv_ref[:, lanes] = gv.astype(BF)


def last_and_back(stream, saved, cotangent, rows8, downs, ups, weights, lengths):
    last = len(saved)
    layers = last + 1
    rows, width = cotangent.shape
    ff = weights.ff
    keys = tuple((name, at) for at in reversed(range(layers)) for name in ("qkv", "out", "up", "down"))
    keys = tuple(key for key in keys if key != ("qkv", 0))
    names = ("q", "k", "v", "o", "lse", "mid", "n1", "rs", "slope", "n2", "r")
    raw = [cotangent, stream, downs, ups]
    for at in reversed(range(last)):
        raw += [saved[at][name] for name in names]

    def body(len_ref, rows_ref, *rest):
        cot_in, x_in, down_in, up_in = rest[:4]
        rest = rest[4:]
        given = [None] * layers
        for at in reversed(range(last)):
            given[at] = dict(zip(names, rest))
            rest = rest[len(names) :]
        bound, rest = weights.bind(keys, rest)
        far, (mine_ref, send_ref, gm_ref), rest = rest[:5], rest[5:8], rest[8:]
        near, rest = rest[:5], rest[5:]
        out_ref, ghid_ref, gq_ref, gk_ref, gv_ref = near
        (sums_ref, wd_ref, wu_ref, wo_ref, wq_ref, cot_ref, g_ref, a_ref, wide_ref, gb_ref, go_ref, bias_ref) = rest[:12]
        down_ref, up_ref = rest[12:14]
        keep = dict(zip(names, rest[14:25]))
        sem, sem_out = rest[25:]

        def give(i, op="start"):
            getattr(pltpu.make_async_copy(near[i], far[i], sem_out.at[i]), op)()

        extra = ("down", "up", "out", "qkv", "cot", "x", "qkv1", "qkv2", "downs", "ups")
        sems = {n: sem.at[i] for i, n in enumerate(names + extra)}

        def fetch(at, *which):
            for name in which:
                copy_in(given[at][name], keep[name], sems[name])

        def take(*which):
            for name in which:
                wait_all(keep[name], sems[name])

        qkv_sem = [sems[name] for name in ("qkv", "qkv1", "qkv2")]
        copy_in(x_in, g_ref, sems["x"])
        copy_in(down_in, down_ref, sems["downs"])
        copy_in(up_in, up_ref, sems["ups"])
        weights.start(bound, ("qkv", last), wq_ref, qkv_sem)
        weights.start(bound, ("out", last), wo_ref, [sems["out"]])
        weights.start(bound, ("up", last), wu_ref, [sems["up"]])
        weights.start(bound, ("down", last), wd_ref, [sems["down"]])
        copy_in(cot_in, cot_ref, sems["cot"])
        bias_ref[...] = mask_bias(len_ref, rows)
        for at in reversed(range(layers)):
            gains = rows_ref[8 * at : 8 * at + 8]
            if at == last:
                wait_all(g_ref, sems["x"])
                keep["r"][...] = g_ref[...].astype(BF)
                wait_all(down_ref, sems["downs"])
                wait_all(up_ref, sems["ups"])
                project(
                    keep["r"][...],
                    down_ref[at],
                    lambda columns: up_ref[last, :, columns],
                    wq_ref,
                    lambda i: wait_all(third(wq_ref, i), qkv_sem[i]),
                    keep["mid"],
                    [keep[name] for name in "qkv"],
                    lambda i: None,
                )
                attend(*[keep[name] for name in ("q", "k", "v", "o", "lse")], bias_ref)
                scale1 = dense_up(
                    lambda j: g_ref[:, j : j + TILE],
                    keep["o"],
                    wo_ref,
                    lambda: wait_all(wo_ref, sems["out"]),
                    wu_ref,
                    lambda j: wait_all(wu_ref, sems["up"]) if j == 0 else None,
                    gains,
                    keep["n1"],
                    wide_ref,
                    gb_ref,
                    keep["slope"],
                    a_ref,
                )
                keep["rs"][...] = jnp.broadcast_to(scale1, (rows, 128))
                wait_all(wd_ref, sems["down"])
                for j in range(0, width, TILE):
                    wide_ref[:, j : j + TILE] += mm(a_ref[...], wd_ref[:, j : j + TILE])
                n2, scale2 = normalize(wide_ref[...])
                out_ref[...] = (n2 * gains[2:3] + gains[3:4]).astype(out_ref.dtype)
                give(0)
                wait_all(cot_ref, sems["cot"])
                incoming = cot_ref[...].astype(F32)
            else:
                take("rs", "n2")
                n2, scale2 = keep["n2"][...].astype(F32), keep["rs"][:, 64:65]
                incoming = g_ref[...]
                wait_all(wd_ref, sems["down"])
                wait_all(wu_ref, sems["up"])
                wait_all(wo_ref, sems["out"])
                take("slope", "n1")
            gz = norm_backward(incoming * gains[2:3], n2, scale2)
            wide_ref[...] = gz
            gb_ref[...] = gz.astype(BF)
            for j in range(0, ff, TILE):
                ga = mm_rt(gb_ref[...], wd_ref[j : j + TILE, :])
                a_ref[:, j : j + TILE] = (ga * keep["slope"][:, j : j + TILE].astype(F32)).astype(BF)
            for j in range(0, width, TILE):
                wide_ref[:, j : j + TILE] += mm_rt(a_ref[...], wu_ref[j : j + TILE, :])
            scale1 = keep["rs"][:, 0:1]
            ghid = norm_backward(wide_ref[...] * gains[0:1], keep["n1"][...].astype(F32), scale1)
            ghid_ref[...] = ghid
            if at == 0:
                give(1)
            gb_ref[...] = ghid.astype(BF)
            for j in range(0, width, TILE):
                go_ref[:, j : j + TILE] = mm_rt(gb_ref[...], wo_ref[j : j + TILE, :]).astype(BF)
            if at > 0:
                weights.start(bound, ("down", at - 1), wd_ref, [sems["down"]])
                fetch(at - 1, "n2", "rs", "slope", "n1")
                weights.start(bound, ("up", at - 1), wu_ref, [sems["up"]])
                weights.start(bound, ("out", at - 1), wo_ref, [sems["out"]])
            if at < last:
                take("q", "k", "v", "lse", "o")
            attend_backward(
                keep["q"], keep["k"], keep["v"], keep["o"], go_ref, keep["lse"], bias_ref, gq_ref, gk_ref, gv_ref
            )
            if at > 0:
                fetch(at - 1, "q", "k", "v", "o", "lse")
            else:
                for i in (2, 3, 4):
                    give(i)
            up = up_ref.at[at]
            gm = mm_rt(gq_ref[...], up[:, :width]) + mm_rt(gv_ref[...], up[:, 2 * width :])
            gm = gm.astype(BF)
            if at < last:
                take("mid", "r")
            base = 32 * at
            sums_ref[base : base + 16] = mm_lt(gm, keep["r"][...])[0:16]
            sums_ref[base + 16 : base + 24] = 2.0 * mm_lt(keep["mid"][...], gq_ref[...])[0:8]
            sums_ref[base + 24 : base + 32] = 2.0 * mm_lt(keep["mid"][...], gv_ref[...])[8:16]
            if at == 0:
                gm_ref[...] = gm
                half = width // 2
                first = lax.axis_index("head") == 0
                left, right = sums_ref[:, :half], sums_ref[:, half:]
                mine_ref[...] = jnp.where(first, left, right)
                send_ref[...] = jnp.where(first, right, left).astype(BF)
                for i in range(5):
                    give(i, "wait")
                continue
            fetch(at - 1, "mid", "r")
            if at < last:
                wait_all(wq_ref, sems["qkv"])
            for j in range(0, width, TILE):
                rs = slice(j, j + TILE)
                total = ghid_ref[:, rs] + mm_rt(gm, down_ref[at, rs, :])
                total += mm_rt(gq_ref[...], wq_ref[rs, :width])
                total += mm_rt(gk_ref[...], wq_ref[rs, width : 2 * width])
                total += mm_rt(gv_ref[...], wq_ref[rs, 2 * width :])
                g_ref[:, rs] = total
            if at > 1:
                weights.start(bound, ("qkv", at - 1), wq_ref, [sems["qkv"]])

    act = sds((rows, width), BF)
    sums = (32 * layers, width // 2)
    outs = (act, sds((rows, width), F32), act, act, act, sds(sums, F32), sds(sums, BF), sds((rows, 128), BF))
    scratch = [pltpu.VMEM(out.shape, out.dtype) for out in outs[:5]]
    scratch += [
        pltpu.VMEM((32 * layers, width), F32),
        pltpu.VMEM((ff, width), BF),
        pltpu.VMEM((width, ff), BF),
        pltpu.VMEM((width, width), BF),
        pltpu.VMEM((width, 3 * width), BF),
        pltpu.VMEM((rows, width), cotangent.dtype),
        pltpu.VMEM((rows, width), F32),
        pltpu.VMEM((rows, ff), BF),
        pltpu.VMEM((rows, width), F32),
        pltpu.VMEM((rows, width), BF),
        pltpu.VMEM((rows, width), BF),
        pltpu.VMEM((rows, rows), F32),
        pltpu.VMEM(downs.shape, BF),
        pltpu.VMEM(ups.shape, BF),
    ]
    scratch += [pltpu.VMEM(saved[0][name].shape, saved[0][name].dtype) for name in names]
    scratch += [pltpu.SemaphoreType.DMA((len(names) + 10,)), pltpu.SemaphoreType.DMA((5,))]
    return kernel_call(
        body,
        outs,
        scratch,
        layers * (6 * rows * width * (2 * width + ff) + 40 * rows * rows * width),
        (lengths,),
        (rows8,),
        raw + weights.leaves(keys),
        raw_outs=5,
    )


def input_grad(ghid, gq, gk, gv, gm, down, weights):
    rows, width = ghid.shape
    keys = (("qkv", 0),)
    given = (gq, gk, gv, gm, down, ghid)

    def body(*rest):
        far, rest = rest[: len(given)], rest[len(given) :]
        bound, rest = weights.bind(keys, rest)
        out_ref, w_ref, sem = rest[0], rest[1], rest[-1]
        near = rest[2:-1]
        gq_ref, gk_ref, gv_ref, gm_ref, down_ref, ghid_ref = near
        weights.start(bound, keys[0], w_ref, [sem.at[0]])
        for i, ref in enumerate(near):
            copy_in(far[i], ref, sem.at[1 + i])
        for i, ref in enumerate(near):
            wait_all(ref, sem.at[1 + i])
        wait_all(w_ref, sem.at[0])
        for j in range(0, width, TILE):
            rs = slice(j, j + TILE)
            total = ghid_ref[:, rs] + mm_rt(gm_ref[...], down_ref[rs, :])
            total += mm_rt(gq_ref[...], w_ref[rs, :width])
            total += mm_rt(gk_ref[...], w_ref[rs, width : 2 * width])
            total += mm_rt(gv_ref[...], w_ref[rs, 2 * width :])
            out_ref[:, rs] = total

    return kernel_call(
        body,
        (sds((rows, width), F32),),
        [pltpu.VMEM((width, 3 * width), BF)]
        + [pltpu.VMEM(v.shape, v.dtype) for v in given]
        + [pltpu.SemaphoreType.DMA((1 + len(given),))],
        6 * rows * width * width,
        (),
        (),
        list(given) + weights.leaves(keys),
    )[0]


def whole_weights(grid, tensors):
    w_query, w_key, w_value, w_out, w_up, w_down = tensors
    groups, places = {}, {}
    half = w_query.shape[2]
    for at in range(w_query.shape[0]):
        qkv = jnp.concatenate([w[at].astype(BF) for w in (w_query, w_key, w_value)], 1)
        qkv = lax.all_gather(qkv, "dp", axis=0, tiled=True)
        qkv = lax.all_gather(qkv, "head", axis=0, tiled=False)
        heads, width = qkv.shape[0], qkv.shape[1]
        qkv = qkv.reshape(heads, width, 3, half).transpose(1, 2, 0, 3).reshape(width, 3 * heads * half)
        groups["qkv", at] = qkv
        for name, w in (("out", w_out), ("up", w_up), ("down", w_down)):
            groups[name, at] = lax.all_gather(w[at].astype(BF), ("dp", "head"), axis=0, tiled=True)
        for name in ("qkv", "out", "up", "down"):
            places[name, at] = ((name, at), ())
    return Gathered(grid, groups, places)


class Chunk:
    def __init__(self, packed, grid):
        self.grid = grid
        self.packed = packed
        self.cut = cut_of(packed.shape[1])

    def spread_z(self, *gates):
        packed = after(self.packed, *gates) if gates else self.packed
        self.line = [packed] + [shift(packed, self.grid, 0, k) for k in range(1, self.grid[0])]
        return self.line[1:]

    def spread_first(self, *gates):
        line = lax.optimization_barrier((*self.line, *gates))[: len(self.line)]
        parts = (jnp.stack([t[:, : self.cut] for t in line]), jnp.stack([t[:, self.cut :] for t in line]))
        self.first = []
        come = []
        for part, axis in zip(parts, (1, 2)):
            moved = [shift(part, self.grid, axis, k) for k in range(1, self.grid[axis])]
            come += moved
            self.first.append([part] + moved)
        return come

    def spread_second(self, *gates):
        split = len(self.first[0])
        flat = (*self.first[0], *self.first[1])
        flat = lax.optimization_barrier((*flat, *gates))[: len(flat)]
        lines = [jnp.stack(flat[:split]), jnp.stack(flat[split:])]
        self.halves = []
        come = []
        for line, axis in zip(lines, (2, 1)):
            moved = [shift(line, self.grid, axis, k) for k in range(1, self.grid[axis])]
            come += moved
            self.halves.append([line] + moved)
        return come

    def swap(self, *gates):
        if gates:
            leaves, tree = jax.tree.flatten(self.halves)
            leaves = lax.optimization_barrier((*leaves, *gates))[: len(leaves)]
            self.halves = jax.tree.unflatten(tree, leaves)
        return [[(own, swap_cores(own)) for own in half] for half in self.halves]


def gather_and_run(chunks, weights, tokens, small, projection, attention, dense):
    def arrive(index, *gates):
        weights.groups[index] = c[index].swap(*gates)

    c = chunks
    c[0].spread_z()
    line1 = c[1].spread_z()
    first0 = c[0].spread_first(c[1].packed)
    line2 = c[2].spread_z(*first0, c[1].packed)
    c[0].spread_second()
    arrive(0)
    first1 = c[1].spread_first()
    q = projection(0, after(tokens, *line1, *small))
    c[1].spread_second(q)
    o = attention(0, line2[0])
    c[2].spread_first(*first1, o)
    arrive(1)
    stream = dense(0, tokens, o)
    c[2].spread_second(stream)
    arrive(2)
    return stream


def sum_over_devices(mine, send, grid):
    total = mine + swap_cores(send).astype(F32)
    nz, ny, nx = grid
    plane = [(0, ky, kx) for ky in range(ny) for kx in range(nx)]
    for steps in (plane[1:], [(k, 0, 0) for k in range(1, nz)]):
        rounded = total.astype(BF)
        parts = [move(rounded, grid, step).astype(F32) for step in steps]
        total = functools.reduce(jnp.add, parts, rounded.astype(F32))
    return total


def pack_chunks(tensors):
    w_query, w_key, w_value, w_out, w_up, w_down = tensors
    layers, rows, half = w_query.shape
    width, ff = 2 * half, w_up.shape[2]
    core = lax.axis_index("head")
    both = jnp.concatenate([w_out, w_up], 2).astype(BF)

    def columns(which):
        return jnp.concatenate(
            [
                lax.dynamic_slice_in_dim(both, which * half, half, 2),
                lax.dynamic_slice_in_dim(both, width + which * (ff // 2), ff // 2, 2),
            ],
            2,
        )

    mine, come = columns(core), swap_cores(columns(1 - core))
    both = jnp.concatenate([jnp.where(core == 0, mine, come), jnp.where(core == 0, come, mine)], 1)
    parts = w_down.shape[1] // rows
    made = {}
    for at in range(layers):
        made["qkv", at] = [w[at].astype(BF) for w in (w_query, w_key, w_value)]
        made["out", at] = [both[at, :, :half]]
        made["up", at] = [both[at, :, half:]]
        made["down", at] = [w_down[at, i * rows : (i + 1) * rows].astype(BF) for i in range(parts)]
    dense = ("out", "up", "down")
    chunks = [[("qkv", 0)], [(name, 0) for name in dense], [(name, 1) for name in ("qkv", *dense)]]
    packs, places = [], {}
    for index, keys in enumerate(chunks):
        lanes = sum(block.shape[1] for key in keys for block in made[key])
        cut, at = cut_of(lanes), 0
        for key in keys:
            items = []
            for run, (wide, placer) in enumerate(tensor_items(key[0], rows, width, ff, parts)):
                for half_at, low, high in ((0, 0, cut), (1, cut, lanes)):
                    start, stop = max(at, low), min(at + wide, high)
                    if start < stop:
                        items.append((half_at, start - low, stop - start, placer(start - at), run))
                at += wide
            places[key] = (index, items)
        packs.append(jnp.concatenate([block for key in keys for block in made[key]], 1))
    return packs, places


def body(
    tokens,
    seq_len,
    w_query,
    w_key,
    w_value,
    w_out,
    w_up,
    w_down,
    a_query,
    b_query,
    a_value,
    b_value,
    ln_gain,
    ln_bias,
    cotangent,
):
    layers, width = w_query.shape[0], tokens.shape[1]
    rank = a_query.shape[2]
    half = b_query.shape[2]
    grid = chip_grid(lax.axis_size("dp"))
    core = lax.axis_index("head")
    tensors = (w_query, w_key, w_value, w_out, w_up, w_down)

    own = jnp.stack([b_query, b_value], 1).astype(BF)
    other = swap_cores(own)
    up_all = jnp.concatenate([jnp.where(core == 0, own, other), jnp.where(core == 0, other, own)], -1)
    pair = jnp.concatenate([a_query, a_value], 2).astype(BF)
    downs = jnp.pad(pair, ((0, 0), (0, 0), (0, 128 - 2 * rank)))
    q_up = jnp.pad(2.0 * up_all[:, 0], ((0, 0), (0, 128 - rank), (0, 0)))
    v_up = jnp.pad(2.0 * up_all[:, 1], ((0, 0), (rank, 128 - 2 * rank), (0, 0)))
    ups = jnp.concatenate([q_up, jnp.zeros_like(q_up), v_up], 2)
    gains = jnp.stack([ln_gain[:, 0], ln_bias[:, 0], ln_gain[:, 1], ln_bias[:, 1]], 1)
    rows8 = jnp.pad(gains, ((0, 0), (0, 4), (0, 0)))

    pieces = w_query.shape[1] % 16 == 0 and lax.axis_size("head") == 2 and layers == 2
    saved = []
    if not pieces:
        weights = whole_weights(grid, tensors)
        weights.ff = w_up.shape[2]
    else:
        packs, places = pack_chunks(tensors)
        chunks = [Chunk(packed, grid) for packed in packs]
        weights = Gathered(grid, {}, places)
        weights.ff = w_up.shape[2]

    def projection(at, stream):
        got = project_forward(stream, downs[at], ups[at], weights, at)
        saved.append(dict(zip(("q", "k", "v", "mid"), got)))
        return got[0]

    def attention(at, *gates):
        q, k, v = (saved[at][name] for name in "qkv")
        o, lse = attend_forward(after(q, *gates) if gates else q, k, v, seq_len)
        saved[at].update(o=o, lse=lse)
        return o

    def dense(at, stream, attended):
        got = dense_forward(stream, attended, rows8[at], weights, at)
        saved[at].update(zip(("n1", "rs", "slope", "out", "n2"), got))
        saved[at]["r"] = stream.astype(BF)
        return saved[at]["out"]

    if not pieces:
        stream = tokens
        for at in range(layers - 1):
            projection(at, stream)
            stream = dense(at, stream, attention(at))
    else:
        stream = gather_and_run(chunks, weights, tokens, (downs, ups, rows8), projection, attention, dense)
    output, ghid, gq, gk, gv, mine, send, gm = last_and_back(
        stream, saved, cotangent, rows8.reshape(8 * layers, width), downs, ups, weights, seq_len
    )
    grad = input_grad(ghid, gq, gk, gv, gm, downs[0], weights)
    total = sum_over_devices(mine, send, grid).reshape(layers, 4, rank, half)
    lower = total[:, :2].reshape(layers * 2 * rank, half)
    far = swap_cores(lower)
    lower = jnp.concatenate([jnp.where(core == 0, lower, far), jnp.where(core == 0, far, lower)], 1)
    lower = lower.reshape(layers, 2, rank, width).transpose(0, 1, 3, 2)
    return (output, grad, lower[:, 0], total[:, 2], lower[:, 1], total[:, 3])


def solution(mesh):
    both = ("dp", "head")
    placed = (
        P(both, None),
        P("dp"),
        P(None, "dp", "head"),
        P(None, "dp", "head"),
        P(None, "dp", "head"),
        P(None, both, None),
        P(None, both, None),
        P(None, both, None),
        P(),
        P(None, None, "head"),
        P(),
        P(None, None, "head"),
        P(),
        P(),
        P(both, None),
    )
    return jax.shard_map(
        body,
        mesh=mesh,
        in_specs=placed,
        out_specs=(
            P(both, None),
            P(both, None),
            P(),
            P(None, None, "head"),
            P(),
            P(None, None, "head"),
        ),
        check_vma=False,
    )
```
